32 devices in a mesh: space: 4 (over y, x), tm: 8 (over z, core).
Axes of the slice: x: 2, y: 2, z: 4, core: 2. Of those that a mesh axis runs over, the one named last changes fastest.
Arguments:
- snapshots: float32 [4096, 4096], P('space', 'tm'), may hold values from -6 to 6
- test_seeds: int32 [2], replicated, may hold values from 0 to 16777215
- block_offsets: int32 [2], replicated, may hold values from 0 to 4095
Outputs:
- residual: float32 [4096, 4096], P('space', 'tm')
- factor: float32 [512, 512], replicated
The draws below stay inside these ranges and needn't reach their ends.
Inputs may be any that keep to these rules, and one draw needn't show every extreme that they name: `test_seeds`: seeds of the two test matrices.
All inputs are finite; a program needn't handle non-finite values.
Results may differ from the reference program's by a relative error of at most 0.0003.
Values sent between devices are 32-bit elements; how exact they have to be, the bound alone decides.
A program may use at most 128 MiB of HBM per device.

```python
import math
import jax
import jax.numpy as jnp
from jax import lax

RANGE = 512
CORANGE = 1024
CELLS = 4096
SNAPS = 4096


def shard_levels(stream_key, dims, shards, least, largest):
    level = 1.0
    for position, blocks in shards:
        steps = jax.random.uniform(jax.random.fold_in(jax.random.fold_in(stream_key, 6), position), (blocks,), jnp.float32, least / len(shards), largest / len(shards))
        level = level * jnp.repeat(jnp.exp(steps), dims[position] // blocks).reshape((-1,) + (1,) * (len(dims) - 1 - position))
    return level


def gaussian(key, shape, scale, reach, split=(), kind=jnp.bfloat16):
    factor_of = shard_levels(key, shape, split, -0.22, 0.18) if split else 1.0
    entries = jax.random.normal(key, shape, jnp.float32) * scale * factor_of
    return jnp.minimum(jnp.maximum(entries, -reach), reach).astype(kind)


def setup_inputs(seed: int = 0) -> dict:
    seeds = jax.random.split(jax.random.key(seed), 4)
    return {
        "snapshots": gaussian(seeds[0], (CELLS, SNAPS), 1.0, 6.0, ((0, 4), (1, 8)), jnp.float32),
        "test_seeds": jax.random.randint(seeds[1], (2,), 0, 16777216).astype(jnp.int32),
        "block_offsets": jax.random.randint(seeds[2], (2,), 0, 4096).astype(jnp.int32),
    }


PRECISE = lax.Precision.HIGHEST

def scramble(values):
    values = jnp.bitwise_xor(values, lax.shift_right_logical(values, jnp.int32(16)))
    values = values * 73244475
    values = jnp.bitwise_xor(values, lax.shift_right_logical(values, jnp.int32(16)))
    values = values * 73244475
    values = jnp.bitwise_xor(values, lax.shift_right_logical(values, jnp.int32(16)))
    return values

def gaussian_table(row_ids, col_ids, seed_value):
    row_hash = scramble(row_ids * 668265261 + seed_value)
    cell_hash = scramble(jnp.bitwise_xor(row_hash[:, None], col_ids[None, :] * 374761393))
    running = jnp.zeros(cell_hash.shape, jnp.float32)
    for stream in range(4):
        hashed = scramble(cell_hash + stream * 625341585)
        running = running + jnp.bitwise_and(hashed, 16777215).astype(jnp.float32) * (1.0 / 16777216.0)
    return (running - 2.0) * math.sqrt(3.0)

def reference(snapshots, test_seeds, block_offsets):
    cell_ids = block_offsets[0] * CELLS + jnp.arange(CELLS, dtype=jnp.int32)
    snap_ids = block_offsets[1] * SNAPS + jnp.arange(SNAPS, dtype=jnp.int32)
    omega_test = gaussian_table(snap_ids, jnp.arange(RANGE, dtype=jnp.int32), test_seeds[0]) / math.sqrt(CELLS * SNAPS)
    psi_test = gaussian_table(cell_ids, jnp.arange(CORANGE, dtype=jnp.int32), test_seeds[1]) / math.sqrt(CELLS)
    range_sketch = jnp.dot(snapshots, omega_test, precision=PRECISE)
    corange_sketch = jnp.dot(psi_test.T, snapshots, precision=PRECISE)
    range_basis, factor = jnp.linalg.qr(range_sketch)
    sign_fix = jnp.where(jnp.diagonal(factor) < 0, -1.0, 1.0).astype(jnp.float32)
    range_basis = range_basis * sign_fix[None, :]
    factor = factor * sign_fix[:, None]
    coupling = jnp.dot(psi_test.T, range_basis, precision=PRECISE)
    normal = jnp.dot(coupling.T, coupling, precision=PRECISE)
    core_factor = jnp.linalg.cholesky(normal)
    projected = jnp.dot(coupling.T, corange_sketch, precision=PRECISE)
    core_matrix = jax.scipy.linalg.cho_solve((core_factor, True), projected)
    residual = snapshots - jnp.dot(range_basis, core_matrix, precision=PRECISE)
    return (residual, factor)
```

```python
import functools
import math

import jax
import jax.numpy as jnp
from jax import lax
from jax.experimental import pallas as pl
from jax.experimental.pallas import tpu as pltpu
from jax.sharding import PartitionSpec as P

RANGE = 512
CORANGE = 1024
BLOCK = 32
GROUP = 8
STRIP = 16

MESH = pl.DeviceIdType.MESH
PRECISE = lax.Precision.HIGHEST
SPLIT = lax.Precision.HIGH


def scramble(values):
    values = jnp.bitwise_xor(values, lax.shift_right_logical(values, jnp.int32(16)))
    values = values * 73244475
    values = jnp.bitwise_xor(values, lax.shift_right_logical(values, jnp.int32(16)))
    values = values * 73244475
    values = jnp.bitwise_xor(values, lax.shift_right_logical(values, jnp.int32(16)))
    return values


def table_strip(row_hash, col_ids, scale):
    cell_hash = scramble(jnp.bitwise_xor(row_hash, col_ids * 374761393))
    total = None
    for stream in range(4):
        hashed = scramble(cell_hash + stream * 625341585) if stream else scramble(cell_hash)
        term = jnp.bitwise_and(hashed, 16777215)
        total = term if total is None else total + term
    return (total - 33554432).astype(jnp.float32) * jnp.float32(scale)


def halves(values):
    high = values.astype(jnp.bfloat16)
    low = (values - high.astype(jnp.float32)).astype(jnp.bfloat16)
    return high, low


def nt(left_side, right_side, precision=None):
    return lax.dot_general(
        left_side, right_side, (((1,), (1,)), ((), ())), precision=precision,
        preferred_element_type=jnp.float32,
    )


def nn(left_side, right_side):
    return jnp.dot(left_side, right_side, preferred_element_type=jnp.float32)


class Ring:
    def __init__(self, place, buffer, send, recv, core_send, core_recv):
        self.__dict__.update(place)
        self.buffer = buffer
        self.sems = (send, recv, core_send, core_recv)
        self.steps = self.ring // 2
        self.started = []
        self.core_copies = []

    def rows(self, piece, half):
        start = self.core * self.half_rows + piece * self.piece_rows + half * self.piece_rows // 2
        return pl.ds(pl.multiple_of(start, 8), self.piece_rows // 2)

    def valid(self, way, step, half):
        return step < self.steps or (step == self.steps and half == way)

    def piece(self, way, hops):
        shift = self.ring - hops if way == 0 else hops
        return lax.rem(self.z + shift, self.ring)

    def copy(self, way, step, half):
        send, recv, _, _ = self.sems
        rows = self.rows(self.piece(way, step - 1), half)
        return pltpu.make_async_remote_copy(
            src_ref=self.buffer.at[rows], dst_ref=self.buffer.at[rows],
            send_sem=send.at[way, step - 1, half], recv_sem=recv.at[way, step - 1, half],
            device_id=self.right if way == 0 else self.left, device_id_type=MESH,
        )

    def to_core(self, way, hops, half):
        _, _, send, recv = self.sems
        rows = self.rows(self.piece(way, hops), half)
        copy = pltpu.make_async_remote_copy(
            src_ref=self.buffer.at[rows], dst_ref=self.buffer.at[rows],
            send_sem=send.at[way, hops, half], recv_sem=recv.at[way, hops, half],
            device_id=self.partner, device_id_type=MESH,
        )
        copy.start()
        self.core_copies.append((way, hops, half, copy))

    def send(self, way, step, half):
        copy = self.copy(way, step, half)
        copy.start()
        self.started.append(copy)

    def start(self):
        for half in range(2):
            for way in range(2):
                self.send(way, 1, half if way == 0 else 1 - half)
        for half in range(2):
            self.to_core(0, 0, half)

    def advance(self, step):
        for turn in range(2):
            for way in range(2):
                half = turn if way == 0 else 1 - turn
                if not self.valid(way, step, half):
                    continue
                self.copy(way, step, half).wait_recv()
                if self.valid(way, step + 1, half):
                    self.send(way, step + 1, half)
                self.to_core(way, step, half)

    def finish(self):
        _, _, send, recv = self.sems
        for way, hops, half, copy in self.core_copies:
            start = (
                (1 - self.core) * self.half_rows
                + self.piece(way, hops) * self.piece_rows
                + half * self.piece_rows // 2
            )
            rows = pl.ds(pl.multiple_of(start, 8), self.piece_rows // 2)
            pltpu.make_async_remote_copy(
                src_ref=self.buffer.at[rows], dst_ref=self.buffer.at[rows],
                send_sem=send.at[way, hops, half], recv_sem=recv.at[way, hops, half],
                device_id=self.partner, device_id_type=MESH,
            ).wait_recv()

    def drain(self):
        for copy in self.started:
            copy.wait_send()
        for _, _, _, copy in self.core_copies:
            copy.wait_send()


class Square:
    def __init__(self, place, source, slots, send, recv):
        self.copies = [
            pltpu.make_async_remote_copy(
                src_ref=source, dst_ref=slots.at[index], send_sem=send.at[index],
                recv_sem=recv.at[index], device_id=peer, device_id_type=MESH,
            )
            for index, peer in enumerate(place["peers"])
        ]

    def start(self):
        for copy in self.copies:
            copy.start()

    def arrive(self):
        for copy in self.copies:
            copy.wait_recv()

    def drain(self):
        for copy in self.copies:
            copy.wait_send()


def sketch_kernel(
    squares, ring, seeds_ref, offsets_ref, a_ref, yt_out, gram_out, normal_out, rhs_out,
    a_hi, a_lo, o_hi, o_lo, p_hi, p_lo, give, got, yc, from_left, from_right, yt, mt, gt,
    m_block, m_slots, g_block, g_slots, w_hi, w_lo, normal, rhs,
    give_send, give_recv, rs_send, rs_recv, y_sems, ycore_sems, m_sems, mcore_sems,
    g_sems, gcore_sems, msq_sems, gsq_sems, out_sems,
):
    space = lax.axis_index("space")
    tm = lax.axis_index("tm")
    core = lax.rem(tm, 2)
    z = lax.div(tm, 2)
    cells, snaps = a_ref.shape
    half_rows = RANGE // 2
    piece_rows = half_rows // ring
    chunk = piece_rows // 2
    steps = ring // 2
    partner = (space, z * 2 + 1 - core)
    right = (space, lax.rem(z + 1, ring) * 2 + core)
    left = (space, lax.rem(z + ring - 1, ring) * 2 + core)
    peers = [(lax.rem(space + index, squares), tm) for index in range(1, squares)]
    place = dict(
        z=z, core=core, ring=ring, half_rows=half_rows, piece_rows=piece_rows,
        partner=partner, right=right, left=left, peers=peers,
    )

    barrier = pltpu.get_barrier_semaphore()
    for device in [partner, right, left] + peers:
        pl.semaphore_signal(barrier, inc=1, device_id=device, device_id_type=MESH)

    snap_ids = (
        offsets_ref[1] * (snaps * ring * 2) + tm * snaps
        + lax.broadcasted_iota(jnp.int32, (1, snaps), 1)
    )
    snap_hash = scramble(snap_ids * 668265261 + seeds_ref[0])
    cell_ids = (
        offsets_ref[0] * (cells * squares) + space * cells
        + lax.broadcasted_iota(jnp.int32, (1, cells), 1)
    )
    cell_hash = scramble(cell_ids * 668265261 + seeds_ref[1])
    omega_scale = math.sqrt(3.0) / 16777216.0 / math.sqrt(cells * squares * snaps * ring * 2)
    psi_scale = math.sqrt(3.0) / 16777216.0 / math.sqrt(cells * squares)

    @pl.loop(0, cells // 128)
    def _(index):
        rows = pl.ds(pl.multiple_of(index * 128, 128), 128)
        a_hi[rows, :], a_lo[rows, :] = halves(a_ref[rows, :])

    def omega(first):
        @pl.loop(0, half_rows // STRIP)
        def _(index):
            base = pl.multiple_of(index * STRIP, STRIP)
            ids = lax.broadcasted_iota(jnp.int32, (STRIP, snaps), 0) + (first + base)
            strip = table_strip(snap_hash, ids, omega_scale)
            o_hi[pl.ds(base, STRIP), :], o_lo[pl.ds(base, STRIP), :] = halves(strip)

    def range_part(target):
        @pl.loop(0, cells // 256)
        def _(index):
            here = pl.ds(pl.multiple_of(index * 256, 256), 256)
            target[:, here] = (
                nt(o_hi[...], a_hi[here, :]) + nt(o_hi[...], a_lo[here, :])
                + nt(o_lo[...], a_hi[here, :])
            )

    def psi(lo, hi):
        @pl.loop(lo // STRIP, hi // STRIP)
        def _(index):
            base = pl.multiple_of(index * STRIP, STRIP)
            ids = lax.broadcasted_iota(jnp.int32, (STRIP, cells), 0) + base
            strip = table_strip(cell_hash, ids, psi_scale)
            p_hi[pl.ds(base, STRIP), :], p_lo[pl.ds(base, STRIP), :] = halves(strip)

    omega((1 - core) * half_rows)
    range_part(give)
    pl.semaphore_wait(barrier, 3 + len(peers))
    order = [steps] + [hop for d in range(steps - 1, 0, -1) for hop in (d, ring - d)] + [0]
    gives = []
    for turn, hop in enumerate(order):
        rows = pl.ds(pl.multiple_of(lax.rem(z + hop, ring) * piece_rows, 8), piece_rows)
        copy = pltpu.make_async_remote_copy(
            src_ref=give.at[rows], dst_ref=got.at[rows], send_sem=give_send.at[turn],
            recv_sem=give_recv.at[turn], device_id=partner, device_id_type=MESH,
        )
        copy.start()
        gives.append((rows, copy))
    omega(core * half_rows)
    range_part(yc)

    def rs_copy(way, step, half, source):
        inbox = from_left if way == 0 else from_right
        return pltpu.make_async_remote_copy(
            src_ref=source, dst_ref=inbox.at[step - 1, half],
            send_sem=rs_send.at[way, step - 1, half], recv_sem=rs_recv.at[way, step - 1, half],
            device_id=right if way == 0 else left, device_id_type=MESH,
        )

    def yc_rows(way, hops, half):
        piece = lax.rem(z + (hops if way == 0 else ring - hops), ring)
        return pl.ds(pl.multiple_of(piece * piece_rows + half * chunk, 8), chunk)

    sent = []

    def rs_send_out(way, step, half):
        if step == steps or (step == steps - 1 and half != way):
            copy = rs_copy(way, step, half, yc.at[yc_rows(way, step, half)])
        else:
            inbox = from_left if way == 0 else from_right
            rs_copy(way, step + 1, half, inbox.at[step, half]).wait_recv()
            inbox[step, half] = inbox[step, half] + yc[yc_rows(way, step, half), :]
            copy = rs_copy(way, step, half, inbox.at[step, half])
        copy.start()
        sent.append(copy)

    for turn, (rows, copy) in enumerate(gives):
        copy.wait_recv()
        yc[rows, :] = yc[rows, :] + got[rows, :]
        if turn == 0:
            for way in range(2):
                rs_send_out(way, steps, way)
        if turn == 2:
            for way in range(2):
                rs_send_out(way, steps - 1, 1 - way)

    quarter = CORANGE // 4
    psi(0, 2 * quarter)
    for step in range(steps - 1, 0, -1):
        for way in range(2):
            rs_send_out(way, step, way)
        if step > 1:
            for way in range(2):
                rs_send_out(way, step - 1, 1 - way)
    psi(2 * quarter, 4 * quarter)
    own_start = core * half_rows + z * piece_rows
    own = pl.ds(pl.multiple_of(own_start, 8), piece_rows)
    for half in range(2):
        for way in range(2):
            rs_copy(way, 1, half, from_left.at[0, half]).wait_recv()
        rows = pl.ds(pl.multiple_of(own_start + half * chunk, 8), chunk)
        yt[rows, :] = yc[yc_rows(0, 0, half), :] + from_left[0, half] + from_right[0, half]
    y_ring = Ring(place, yt, y_sems.at[0], y_sems.at[1], ycore_sems.at[0], ycore_sems.at[1])
    y_ring.start()

    mine_hi, mine_lo = halves(yt[own, :])
    both = jnp.concatenate([mine_hi, mine_lo], axis=0)
    for tile in range(CORANGE // 256):
        here = pl.ds(tile * 256, 256)
        high = nt(both, p_hi[here, :])
        m_block[:, here] = high[:piece_rows] + high[piece_rows:] + nt(mine_hi, p_lo[here, :])
    m_square = Square(place, m_block, m_slots, msq_sems.at[0], msq_sems.at[1])
    m_square.start()

    for step in range(1, steps):
        y_ring.advance(step)

    def corange(lo, hi):
        @pl.loop(lo // 256, hi // 256)
        def _(index):
            here = pl.ds(pl.multiple_of(index * 256, 256), 256)
            part = (
                nn(p_hi[here, :], a_hi[...]) + nn(p_hi[here, :], a_lo[...])
                + nn(p_lo[here, :], a_hi[...])
            )
            w_hi[here, :], w_lo[here, :] = halves(part)

    corange(0, CORANGE)
    m_square.arrive()
    total = m_block[...]
    for index in range(squares - 1):
        total = total + m_slots[index]
    mt[own, :] = total
    m_ring = Ring(place, mt, m_sems.at[0], m_sems.at[1], mcore_sems.at[0], mcore_sems.at[1])
    m_ring.start()
    y_ring.advance(steps)
    y_ring.finish()
    y_store = pltpu.make_async_copy(yt, yt_out, out_sems.at[0])
    y_store.start()
    g_block[...] = nt(yt[own, :], yt[...], PRECISE)
    g_square = Square(place, g_block, g_slots, gsq_sems.at[0], gsq_sems.at[1])
    g_square.start()
    for step in range(1, steps):
        m_ring.advance(step)
    g_square.arrive()
    total = g_block[...]
    for index in range(squares - 1):
        total = total + g_slots[index]
    gt[own, :] = total
    m_ring.advance(steps)
    g_ring = Ring(place, gt, g_sems.at[0], g_sems.at[1], gcore_sems.at[0], gcore_sems.at[1])
    g_ring.start()
    m_ring.finish()

    @pl.loop(0, RANGE // 256)
    def _(index):
        here = pl.ds(pl.multiple_of(index * 256, 256), 256)
        normal[here, :] = nt(mt[here, :], mt[...], PRECISE)

    n_store = pltpu.make_async_copy(normal, normal_out, out_sems.at[1])
    n_store.start()
    for step in range(1, steps):
        g_ring.advance(step)

    @pl.loop(0, RANGE // 256)
    def _(index):
        here = pl.ds(pl.multiple_of(index * 256, 256), 256)
        m_hi, m_lo = halves(mt[here, :])
        rhs[here, :] = nn(m_hi, w_hi[...]) + nn(m_hi, w_lo[...]) + nn(m_lo, w_hi[...])

    r_store = pltpu.make_async_copy(rhs, rhs_out, out_sems.at[2])
    r_store.start()
    g_ring.advance(steps)
    g_ring.finish()
    g_store = pltpu.make_async_copy(gt, gram_out, out_sems.at[3])
    g_store.start()

    for _, copy in gives:
        copy.wait_send()
    for copy in sent:
        copy.wait_send()
    for group in (y_ring, m_ring, g_ring, m_square, g_square):
        group.drain()
    for copy in (y_store, n_store, r_store, g_store):
        copy.wait()


def sketch(snapshots, test_seeds, block_offsets):
    cells, snaps = snapshots.shape
    squares = lax.axis_size("space")
    ring = lax.axis_size("tm") // 2
    half_rows = RANGE // 2
    piece_rows = half_rows // ring
    f32, bf16 = jnp.float32, jnp.bfloat16
    dma = pltpu.SemaphoreType.DMA
    ring_sems = [dma((2, 2, ring // 2, 2)), dma((2, 2, ring // 2 + 1, 2))]
    scratch = [
        pltpu.VMEM((cells, snaps), bf16), pltpu.VMEM((cells, snaps), bf16),
        pltpu.VMEM((half_rows, snaps), bf16), pltpu.VMEM((half_rows, snaps), bf16),
        pltpu.VMEM((CORANGE, cells), bf16), pltpu.VMEM((CORANGE, cells), bf16),
        pltpu.VMEM((half_rows, cells), f32), pltpu.VMEM((half_rows, cells), f32),
        pltpu.VMEM((half_rows, cells), f32),
        pltpu.VMEM((ring // 2, 2, piece_rows // 2, cells), f32),
        pltpu.VMEM((ring // 2, 2, piece_rows // 2, cells), f32),
        pltpu.VMEM((RANGE, cells), f32), pltpu.VMEM((RANGE, CORANGE), f32),
        pltpu.VMEM((RANGE, RANGE), f32),
        pltpu.VMEM((piece_rows, CORANGE), f32),
        pltpu.VMEM((squares - 1, piece_rows, CORANGE), f32),
        pltpu.VMEM((piece_rows, RANGE), f32),
        pltpu.VMEM((squares - 1, piece_rows, RANGE), f32),
        pltpu.VMEM((CORANGE, snaps), bf16), pltpu.VMEM((CORANGE, snaps), bf16),
        pltpu.VMEM((RANGE, RANGE), f32), pltpu.VMEM((RANGE, snaps), f32),
        dma((ring,)), dma((ring,)), dma((2, ring // 2, 2)), dma((2, ring // 2, 2)),
        *ring_sems, *ring_sems, *ring_sems,
        dma((2, squares - 1)), dma((2, squares - 1)), dma((4,)),
    ]
    flops = 2 * 3 * cells * snaps * (RANGE + CORANGE) + 2 * 9 * RANGE * RANGE * CORANGE
    return pl.pallas_call(
        functools.partial(sketch_kernel, squares, ring),
        out_shape=(
            jax.ShapeDtypeStruct((RANGE, cells), f32),
            jax.ShapeDtypeStruct((RANGE, RANGE), f32),
            jax.ShapeDtypeStruct((RANGE, RANGE), f32),
            jax.ShapeDtypeStruct((RANGE, snaps), f32),
        ),
        in_specs=[
            pl.BlockSpec(memory_space=pltpu.SMEM), pl.BlockSpec(memory_space=pltpu.SMEM),
            pl.BlockSpec(memory_space=pltpu.VMEM),
        ],
        out_specs=(pl.BlockSpec(memory_space=pl.ANY),) * 4,
        scratch_shapes=scratch,
        compiler_params=pltpu.CompilerParams(
            collective_id=0, has_side_effects=True, vmem_limit_bytes=48 * 1024 * 1024
        ),
        cost_estimate=pl.CostEstimate(
            flops=flops, bytes_accessed=8 * cells * snaps, transcendentals=0
        ),
        name="sketch",
    )(test_seeds, block_offsets, snapshots)


def gram_dot(left_side, right_side):
    return lax.dot_general(
        left_side, right_side, (((0,), (0,)), ((), ())), precision=PRECISE,
        preferred_element_type=jnp.float32,
    )


def dot(left_side, right_side):
    return jnp.dot(
        left_side, right_side, precision=PRECISE, preferred_element_type=jnp.float32
    )


def eliminate(blocks):
    size = blocks[0].shape[0]
    row_id = lax.broadcasted_iota(jnp.int32, (size, size), 0)
    col_id = lax.broadcasted_iota(jnp.int32, (size, size), 1)
    eye = jnp.where(row_id == col_id, 1.0, 0.0).astype(jnp.float32)
    work = [(block, eye) for block in blocks]
    for start in range(0, size, GROUP):
        columns = [
            [
                jnp.broadcast_to(block[:, start + j : start + j + 1], (size, size))
                for j in range(GROUP)
            ]
            for block, _ in work
        ]
        for j in range(GROUP):
            step = start + j
            later = []
            for (block, inverse), column in zip(work, columns):
                below = jnp.where(row_id > step, column[j], 0.0)
                share = below * (1.0 / column[j][step : step + 1, :])
                for i in range(j + 1, GROUP):
                    column[i] = column[i] - share * column[i][step : step + 1, :]
                later.append(
                    (
                        block - share * block[step : step + 1, :],
                        inverse - share * inverse[step : step + 1, :],
                    )
                )
            work = later
    factors = []
    for block, inverse in work:
        diagonal = jnp.sum(jnp.where(row_id == col_id, block, 0.0), axis=1, keepdims=True)
        factors.append(inverse / jnp.sqrt(diagonal))
    return factors


def factor_kernel(gram_ref, normal_ref, factor_ref, out_ref, g, s):
    n = gram_ref.shape[0]
    tile = 128

    def identity(shape):
        rows = lax.broadcasted_iota(jnp.int32, shape, 0)
        cols = lax.broadcasted_iota(jnp.int32, shape, 1)
        return jnp.where(rows == cols, 1.0, 0.0).astype(jnp.float32)

    g[...] = gram_ref[...]
    s[:, :n] = normal_ref[...]
    s[:, n:] = identity((n, n))

    @pl.loop(0, n // tile)
    def _(index):
        base = pl.multiple_of(index * tile, tile)
        here = pl.ds(base, tile)
        works = [
            jnp.concatenate([ref[here, here], identity((tile, tile))], axis=1) for ref in (g, s)
        ]
        done = [[], []]
        for lo in range(0, tile, BLOCK):
            smalls = eliminate([work[:BLOCK, lo : lo + BLOCK] for work in works])
            for place in range(2):
                rows = dot(smalls[place], works[place][:BLOCK])
                done[place].append(rows[:, tile:])
                if lo + BLOCK < tile:
                    works[place] = works[place][BLOCK:] - gram_dot(
                        rows[:, lo + BLOCK : tile], rows
                    )
        g_panel = dot(jnp.concatenate(done[0], axis=0), g[here, :])
        s_panel = dot(jnp.concatenate(done[1], axis=0), s[here, :])
        rows = lax.broadcasted_iota(jnp.int32, g_panel.shape, 0) + base
        cols = lax.broadcasted_iota(jnp.int32, g_panel.shape, 1)
        factor_ref[here, :] = jnp.where(cols >= rows, g_panel, 0.0)
        after = cols >= base + tile
        g[...] -= gram_dot(jnp.where(after, g_panel, 0.0), g_panel)
        s[...] -= gram_dot(jnp.where(after, s_panel[:, :n], 0.0), s_panel)
        s[here, :] = s_panel

    out_ref[...] = gram_dot(s[:, n:], s[:, n:])


def factor_and_invert(gram, normal):
    n = gram.shape[0]
    return pl.pallas_call(
        factor_kernel,
        out_shape=(jax.ShapeDtypeStruct((n, n), jnp.float32),) * 2,
        in_specs=[pl.BlockSpec(memory_space=pltpu.VMEM)] * 2,
        out_specs=(pl.BlockSpec(memory_space=pltpu.VMEM),) * 2,
        scratch_shapes=[
            pltpu.VMEM((n, n), jnp.float32),
            pltpu.VMEM((n, 2 * n), jnp.float32),
        ],
        compiler_params=pltpu.CompilerParams(vmem_limit_bytes=40 * 1024 * 1024),
        cost_estimate=pl.CostEstimate(
            flops=40 * n * n * n, bytes_accessed=20 * n * n, transcendentals=0
        ),
        name="factor_and_invert",
    )(gram, normal)


def local(snapshots, test_seeds, block_offsets):
    range_t, gram, normal, rhs = sketch(snapshots, test_seeds, block_offsets)
    rhs = lax.psum(rhs, "space")
    factor, inverse = factor_and_invert(gram, normal)
    weights = jnp.dot(inverse, rhs, precision=PRECISE)
    residual = snapshots - lax.dot_general(
        range_t, weights, (((0,), (0,)), ((), ())), precision=SPLIT
    )
    return (residual, factor)


def solution(mesh):
    return jax.shard_map(
        local,
        mesh=mesh,
        in_specs=(P("space", "tm"), P(), P()),
        out_specs=(P("space", "tm"), P()),
        check_vma=False,
    )
```

```python
import functools
import math
import types

import jax
import jax.numpy as jnp
from jax import lax
from jax.experimental import pallas as pl
from jax.experimental.pallas import tpu as pltpu
from jax.sharding import PartitionSpec as P

RANGE = 512
CORANGE = 1024
BLOCK = 32
GROUP = 8
STRIP = 16
CHUNKS = 8

MESH = pl.DeviceIdType.MESH
PRECISE = lax.Precision.HIGHEST
SPLIT = lax.Precision.HIGH


def scramble(values):
    values = jnp.bitwise_xor(values, lax.shift_right_logical(values, jnp.int32(16)))
    values = values * 73244475
    values = jnp.bitwise_xor(values, lax.shift_right_logical(values, jnp.int32(16)))
    values = values * 73244475
    values = jnp.bitwise_xor(values, lax.shift_right_logical(values, jnp.int32(16)))
    return values


def table_strip(row_hash, col_ids, scale):
    cell_hash = scramble(jnp.bitwise_xor(row_hash, col_ids * 374761393))
    total = None
    for stream in range(4):
        hashed = scramble(cell_hash + stream * 625341585) if stream else scramble(cell_hash)
        term = jnp.bitwise_and(hashed, 16777215)
        total = term if total is None else total + term
    return (total - 33554432).astype(jnp.float32) * jnp.float32(scale)


def halves(values):
    high = values.astype(jnp.bfloat16)
    low = (values - high.astype(jnp.float32)).astype(jnp.bfloat16)
    return high, low


def nt(left_side, right_side, precision=None):
    return lax.dot_general(
        left_side, right_side, (((1,), (1,)), ((), ())), precision=precision,
        preferred_element_type=jnp.float32,
    )


def nn(left_side, right_side):
    return jnp.dot(left_side, right_side, preferred_element_type=jnp.float32)


class Shared:
    def __init__(self, place, block, slots, target, first, sems, core_sems):
        self.__dict__.update(vars(place))
        self.block, self.slots, self.target = block, slots, target
        self.sems, self.core_sems = sems, core_sems
        self.count = block.shape[0]
        self.rows = self.count // self.squares
        self.mine = self.core * (RANGE // 2) + first
        self.theirs = (1 - self.core) * (RANGE // 2) + first
        self.sends = []

    def part(self, base, index):
        return pl.ds(pl.multiple_of(base + index * self.rows, 8), self.rows)

    def copy(self, stage, hop, source, target):
        device = (lax.rem(self.space + hop, self.squares), self.tm)
        return pltpu.make_async_remote_copy(
            src_ref=source, dst_ref=target, send_sem=self.sems.at[stage, 0, hop - 1],
            recv_sem=self.sems.at[stage, 1, hop - 1], device_id=device, device_id_type=MESH,
        )

    def scatter(self):
        for hop in range(1, self.squares):
            rows = self.part(0, lax.rem(self.space + hop, self.squares))
            copy = self.copy(0, hop, self.block.at[rows], self.slots.at[hop - 1])
            copy.start()
            self.sends.append(copy)

    def reduce(self):
        for copy in list(self.sends):
            copy.wait_recv()
        total = self.block[self.part(0, self.space), :]
        for hop in range(1, self.squares):
            total = total + self.slots[hop - 1]
        own = self.part(self.mine, self.space)
        self.target[own, :] = total
        self.gathers = []
        for hop in range(1, self.squares):
            copy = self.copy(1, hop, self.target.at[own], self.target.at[own])
            copy.start()
            self.gathers.append(copy)

    def collect(self):
        for hop in range(1, self.squares):
            rows = self.part(self.mine, lax.rem(self.space + self.squares - hop, self.squares))
            self.copy(1, hop, self.target.at[rows], self.target.at[rows]).wait_recv()
        self.pass_on = core_copy(self, self.target, self.mine, self.count, self.core_sems)
        self.pass_on.start()

    def complete(self):
        core_copy(self, self.target, self.theirs, self.count, self.core_sems).wait_recv()

    def drain(self):
        for copy in self.sends + self.gathers + [self.pass_on]:
            copy.wait_send()


def core_copy(place, buffer, first, count, sems):
    rows = pl.ds(pl.multiple_of(first, 8), count)
    return pltpu.make_async_remote_copy(
        src_ref=buffer.at[rows], dst_ref=buffer.at[rows], send_sem=sems.at[0],
        recv_sem=sems.at[1], device_id=place.partner, device_id_type=MESH,
    )


def sketch_kernel(
    squares, line, seeds_ref, offsets_ref, a_ref, yt_out, gram_out, normal_out, rhs_out,
    a_hi, a_lo, o_hi, o_lo, p_hi, p_lo, give, got, own_range, yc, from_left, from_right, to_left,
    yt, mt, gt, m_block, m_slots, g_block, g_slots, w_hi, w_lo, normal, rhs,
    give_sems, line_sems, ycore_sems, m_sems, mcore_sems, g_sems, gcore_sems, out_sems,
):
    space = lax.axis_index("space")
    tm = lax.axis_index("tm")
    core = lax.rem(tm, 2)
    z = lax.div(tm, 2)
    cells, snaps = a_ref.shape
    half_rows = RANGE // 2
    chunk = half_rows // CHUNKS
    groups, group_rows, _ = m_block.shape
    per_group = group_rows // chunk
    partner = (space, z * 2 + 1 - core)
    right = (space, lax.rem(z + 1, line) * 2 + core)
    left = (space, lax.rem(z + line - 1, line) * 2 + core)
    peers = [(lax.rem(space + index, squares), tm) for index in range(1, squares)]
    place = types.SimpleNamespace(
        space=space, tm=tm, core=core, squares=squares, partner=partner
    )

    barrier = pltpu.get_barrier_semaphore()
    for device in [partner, right, left] + peers:
        pl.semaphore_signal(barrier, inc=1, device_id=device, device_id_type=MESH)

    snap_ids = (
        offsets_ref[1] * (snaps * line * 2) + tm * snaps
        + lax.broadcasted_iota(jnp.int32, (1, snaps), 1)
    )
    snap_hash = scramble(snap_ids * 668265261 + seeds_ref[0])
    cell_ids = (
        offsets_ref[0] * (cells * squares) + space * cells
        + lax.broadcasted_iota(jnp.int32, (1, cells), 1)
    )
    cell_hash = scramble(cell_ids * 668265261 + seeds_ref[1])
    omega_scale = math.sqrt(3.0) / 16777216.0 / math.sqrt(cells * squares * snaps * line * 2)
    psi_scale = math.sqrt(3.0) / 16777216.0 / math.sqrt(cells * squares)

    @pl.loop(0, cells // 128)
    def _(index):
        rows = pl.ds(pl.multiple_of(index * 128, 128), 128)
        a_hi[rows, :], a_lo[rows, :] = halves(a_ref[rows, :])

    half_range = half_rows // 2

    def range_part(target, owner, turn):
        offset = turn * half_range

        @pl.loop(0, half_range // STRIP)
        def _(index):
            base = pl.multiple_of(index * STRIP, STRIP)
            ids = lax.broadcasted_iota(jnp.int32, (STRIP, snaps), 0) + (
                owner * half_rows + offset + base
            )
            strip = table_strip(snap_hash, ids, omega_scale)
            o_hi[pl.ds(base, STRIP), :], o_lo[pl.ds(base, STRIP), :] = halves(strip)

        @pl.loop(0, cells // 512)
        def _(index):
            here = pl.ds(pl.multiple_of(index * 512, 512), 512)
            target[offset : offset + half_range, here] = (
                nt(o_hi[...], a_hi[here, :]) + nt(o_hi[...], a_lo[here, :])
                + nt(o_lo[...], a_hi[here, :])
            )

    def psi(lo, hi):
        @pl.loop(lo // STRIP, hi // STRIP)
        def _(index):
            base = pl.multiple_of(index * STRIP, STRIP)
            ids = lax.broadcasted_iota(jnp.int32, (STRIP, cells), 0) + base
            strip = table_strip(cell_hash, ids, psi_scale)
            p_hi[pl.ds(base, STRIP), :], p_lo[pl.ds(base, STRIP), :] = halves(strip)

    def line_copy(way, index, source):
        target = from_left if way == 0 else from_right
        return pltpu.make_async_remote_copy(
            src_ref=source, dst_ref=target.at[index], send_sem=line_sems.at[way, 0, index],
            recv_sem=line_sems.at[way, 1, index],
            device_id=right if way == 0 else left, device_id_type=MESH,
        )

    gives = []
    per_turn = CHUNKS // 2
    for turn in range(2):
        range_part(give, 1 - core, turn)
        if turn == 0:
            pl.semaphore_wait(barrier, 3 + len(peers))
        rows = pl.ds(turn * half_range, half_range)
        copy = pltpu.make_async_remote_copy(
            src_ref=give.at[rows], dst_ref=got.at[rows], send_sem=give_sems.at[0, turn],
            recv_sem=give_sems.at[1, turn], device_id=partner, device_id_type=MESH,
        )
        copy.start()
        gives.append(copy)
        range_part(own_range, core, turn)
        copy.wait_recv()
        for index in range(turn * per_turn, (turn + 1) * per_turn):
            rows = pl.ds(index * chunk, chunk)
            yc[index] = own_range[rows, :] + got[rows, :]

            @pl.when(z == 0)
            def _():
                line_copy(0, index, yc.at[index]).start()

            @pl.when(z == line - 1)
            def _():
                line_copy(1, index, yc.at[index]).start()

    def line_step(step):
        index = step - z

        @pl.when((z > 0) & (index >= 0) & (index < CHUNKS))
        def _():
            line_copy(0, index, yc.at[index]).wait_recv()
            from_left[index] = from_left[index] + yc[index]

            @pl.when(z < line - 1)
            def _():
                line_copy(0, index, from_left.at[index]).start()

        other = step - (line - 1 - z)

        @pl.when((z < line - 1) & (other >= 0) & (other < CHUNKS))
        def _():
            line_copy(1, other, yc.at[other]).wait_recv()

            @pl.when(z > 0)
            def _():
                to_left[other] = from_right[other] + yc[other]
                line_copy(1, other, to_left.at[other]).start()

        done = step - (line - 1)
        if 0 <= done < CHUNKS:
            rows = pl.ds(pl.multiple_of(core * half_rows + done * chunk, 8), chunk)

            @pl.when(z == 0)
            def _():
                yt[rows, :] = yc[done] + from_right[done]

            @pl.when(z == line - 1)
            def _():
                yt[rows, :] = from_left[done]

            @pl.when((z > 0) & (z < line - 1))
            def _():
                yt[rows, :] = from_left[done] + from_right[done]

    def corange(lo, hi):
        for start in range(lo, hi, 256):
            here = pl.ds(start, 256)
            part = (
                nn(p_hi[here, :], a_hi[...]) + nn(p_hi[here, :], a_lo[...])
                + nn(p_lo[here, :], a_hi[...])
            )
            w_hi[here, :], w_lo[here, :] = halves(part)

    y_pass, shared = [], []

    def couple(group):
        first = group * group_rows
        copy = core_copy(place, yt, core * half_rows + first, group_rows, ycore_sems.at[group])
        copy.start()
        y_pass.append(copy)
        rows = pl.ds(pl.multiple_of(core * half_rows + first, 8), group_rows)
        high, low = halves(yt[rows, :])
        both = jnp.concatenate([high, low], axis=0)
        for tile in range(CORANGE // 256):
            here = pl.ds(tile * 256, 256)
            most = nt(both, p_hi[here, :])
            m_block[group, :, here] = (
                most[:group_rows] + most[group_rows:] + nt(high, p_lo[here, :])
            )
        total = Shared(
            place, m_block.at[group], m_slots.at[group], mt, first, m_sems.at[group],
            mcore_sems.at[group],
        )
        total.scatter()
        shared.append(total)

    steps = list(range(1, CHUNKS + line - 1))
    strips = CORANGE // 8
    for turn in range(8):
        psi(turn * strips, (turn + 1) * strips)
        if turn in (1, 4, 7):
            line_step(steps.pop(0))
    for group in range(groups):
        last = (group + 1) * per_group - 1 + line - 1
        while steps and steps[0] <= last:
            line_step(steps.pop(0))
        couple(group)
        if group >= 1:
            shared[group - 1].reduce()
        if group >= 2:
            shared[group - 2].collect()
        if group < groups - 1:
            corange(CORANGE // groups * group, CORANGE // groups * (group + 1))
    for group in range(groups):
        rows = (1 - core) * half_rows + group * group_rows
        core_copy(place, yt, rows, group_rows, ycore_sems.at[group]).wait_recv()
    y_store = pltpu.make_async_copy(yt, yt_out, out_sems.at[0])
    y_store.start()
    mine = pl.ds(pl.multiple_of(core * half_rows, 8), half_rows)
    g_block[...] = nt(yt[mine, :], yt[...], PRECISE)
    g_shared = Shared(place, g_block, g_slots, gt, 0, g_sems, gcore_sems)
    shared[groups - 1].reduce()
    g_shared.scatter()
    shared[groups - 2].collect()
    corange(CORANGE // groups * (groups - 1), CORANGE)
    shared[groups - 1].collect()
    g_shared.reduce()
    for total in shared:
        total.complete()

    @pl.loop(0, RANGE // 256)
    def _(index):
        here = pl.ds(pl.multiple_of(index * 256, 256), 256)
        normal[here, :] = nt(mt[here, :], mt[...], PRECISE)

    n_store = pltpu.make_async_copy(normal, normal_out, out_sems.at[1])
    n_store.start()
    g_shared.collect()

    @pl.loop(0, RANGE // 256)
    def _(index):
        here = pl.ds(pl.multiple_of(index * 256, 256), 256)
        m_hi, m_lo = halves(mt[here, :])
        rhs[here, :] = nn(m_hi, w_hi[...]) + nn(m_hi, w_lo[...]) + nn(m_lo, w_hi[...])

    r_store = pltpu.make_async_copy(rhs, rhs_out, out_sems.at[2])
    r_store.start()
    g_shared.complete()
    g_store = pltpu.make_async_copy(gt, gram_out, out_sems.at[3])
    g_store.start()

    for copy in gives + y_pass:
        copy.wait_send()
    for total in shared + [g_shared]:
        total.drain()

    @pl.when(z < line - 1)
    def _():
        for index in range(CHUNKS):
            line_copy(0, index, yc.at[index]).wait_send()

    @pl.when(z > 0)
    def _():
        for index in range(CHUNKS):
            line_copy(1, index, yc.at[index]).wait_send()

    for copy in (y_store, n_store, r_store, g_store):
        copy.wait()


def sketch(snapshots, test_seeds, block_offsets):
    cells, snaps = snapshots.shape
    squares = lax.axis_size("space")
    line = lax.axis_size("tm") // 2
    half_rows = RANGE // 2
    chunk = half_rows // CHUNKS
    group_rows = max(half_rows // 4, 8 * squares)
    groups = half_rows // group_rows
    f32, bf16 = jnp.float32, jnp.bfloat16
    dma = pltpu.SemaphoreType.DMA
    scratch = [
        pltpu.VMEM((cells, snaps), bf16), pltpu.VMEM((cells, snaps), bf16),
        pltpu.VMEM((half_rows // 2, snaps), bf16), pltpu.VMEM((half_rows // 2, snaps), bf16),
        pltpu.VMEM((CORANGE, cells), bf16), pltpu.VMEM((CORANGE, cells), bf16),
        pltpu.VMEM((half_rows, cells), f32), pltpu.VMEM((half_rows, cells), f32),
        pltpu.VMEM((half_rows, cells), f32),
        pltpu.VMEM((CHUNKS, chunk, cells), f32), pltpu.VMEM((CHUNKS, chunk, cells), f32),
        pltpu.VMEM((CHUNKS, chunk, cells), f32), pltpu.VMEM((CHUNKS, chunk, cells), f32),
        pltpu.VMEM((RANGE, cells), f32), pltpu.VMEM((RANGE, CORANGE), f32),
        pltpu.VMEM((RANGE, RANGE), f32),
        pltpu.VMEM((groups, group_rows, CORANGE), f32),
        pltpu.VMEM((groups, squares - 1, group_rows // squares, CORANGE), f32),
        pltpu.VMEM((half_rows, RANGE), f32),
        pltpu.VMEM((squares - 1, half_rows // squares, RANGE), f32),
        pltpu.VMEM((CORANGE, snaps), bf16), pltpu.VMEM((CORANGE, snaps), bf16),
        pltpu.VMEM((RANGE, RANGE), f32), pltpu.VMEM((RANGE, snaps), f32),
        dma((2, 2)), dma((2, 2, CHUNKS)), dma((groups, 2)),
        dma((groups, 2, 2, squares - 1)), dma((groups, 2)),
        dma((2, 2, squares - 1)), dma((2,)), dma((4,)),
    ]
    flops = 2 * 3 * cells * snaps * (RANGE + CORANGE) + 2 * 9 * RANGE * RANGE * CORANGE
    return pl.pallas_call(
        functools.partial(sketch_kernel, squares, line),
        out_shape=(
            jax.ShapeDtypeStruct((RANGE, cells), f32),
            jax.ShapeDtypeStruct((RANGE, RANGE), f32),
            jax.ShapeDtypeStruct((RANGE, RANGE), f32),
            jax.ShapeDtypeStruct((RANGE, snaps), f32),
        ),
        in_specs=[
            pl.BlockSpec(memory_space=pltpu.SMEM), pl.BlockSpec(memory_space=pltpu.SMEM),
            pl.BlockSpec(memory_space=pltpu.VMEM),
        ],
        out_specs=(pl.BlockSpec(memory_space=pl.ANY),) * 4,
        scratch_shapes=scratch,
        compiler_params=pltpu.CompilerParams(
            collective_id=0, has_side_effects=True, vmem_limit_bytes=48 * 1024 * 1024
        ),
        cost_estimate=pl.CostEstimate(
            flops=flops, bytes_accessed=8 * cells * snaps, transcendentals=0
        ),
        name="sketch",
    )(test_seeds, block_offsets, snapshots)


def gram_dot(left_side, right_side):
    return lax.dot_general(
        left_side, right_side, (((0,), (0,)), ((), ())), precision=PRECISE,
        preferred_element_type=jnp.float32,
    )


def dot(left_side, right_side):
    return jnp.dot(
        left_side, right_side, precision=PRECISE, preferred_element_type=jnp.float32
    )


def eliminate(blocks):
    size = blocks[0].shape[0]
    row_id = lax.broadcasted_iota(jnp.int32, (size, size), 0)
    col_id = lax.broadcasted_iota(jnp.int32, (size, size), 1)
    eye = jnp.where(row_id == col_id, 1.0, 0.0).astype(jnp.float32)
    work = [(block, eye) for block in blocks]
    for start in range(0, size, GROUP):
        columns = [
            [
                jnp.broadcast_to(block[:, start + j : start + j + 1], (size, size))
                for j in range(GROUP)
            ]
            for block, _ in work
        ]
        for j in range(GROUP):
            step = start + j
            later = []
            for (block, inverse), column in zip(work, columns):
                below = jnp.where(row_id > step, column[j], 0.0)
                share = below * (1.0 / column[j][step : step + 1, :])
                for i in range(j + 1, GROUP):
                    column[i] = column[i] - share * column[i][step : step + 1, :]
                later.append(
                    (
                        block - share * block[step : step + 1, :],
                        inverse - share * inverse[step : step + 1, :],
                    )
                )
            work = later
    factors = []
    for block, inverse in work:
        diagonal = jnp.sum(jnp.where(row_id == col_id, block, 0.0), axis=1, keepdims=True)
        factors.append(inverse / jnp.sqrt(diagonal))
    return factors


def factor_kernel(gram_ref, normal_ref, factor_ref, out_ref, g, s):
    n = gram_ref.shape[0]
    tile = 128

    def identity(shape):
        rows = lax.broadcasted_iota(jnp.int32, shape, 0)
        cols = lax.broadcasted_iota(jnp.int32, shape, 1)
        return jnp.where(rows == cols, 1.0, 0.0).astype(jnp.float32)

    g[...] = gram_ref[...]
    s[:, :n] = normal_ref[...]
    s[:, n:] = identity((n, n))

    @pl.loop(0, n // tile)
    def _(index):
        base = pl.multiple_of(index * tile, tile)
        here = pl.ds(base, tile)
        works = [
            jnp.concatenate([ref[here, here], identity((tile, tile))], axis=1) for ref in (g, s)
        ]
        done = [[], []]
        for lo in range(0, tile, BLOCK):
            smalls = eliminate([work[:BLOCK, lo : lo + BLOCK] for work in works])
            for place in range(2):
                rows = dot(smalls[place], works[place][:BLOCK])
                done[place].append(rows[:, tile:])
                if lo + BLOCK < tile:
                    works[place] = works[place][BLOCK:] - gram_dot(
                        rows[:, lo + BLOCK : tile], rows
                    )
        g_panel = dot(jnp.concatenate(done[0], axis=0), g[here, :])
        s_panel = dot(jnp.concatenate(done[1], axis=0), s[here, :])
        rows = lax.broadcasted_iota(jnp.int32, g_panel.shape, 0) + base
        cols = lax.broadcasted_iota(jnp.int32, g_panel.shape, 1)
        factor_ref[here, :] = jnp.where(cols >= rows, g_panel, 0.0)
        after = cols >= base + tile
        g[...] -= gram_dot(jnp.where(after, g_panel, 0.0), g_panel)
        s[...] -= gram_dot(jnp.where(after, s_panel[:, :n], 0.0), s_panel)
        s[here, :] = s_panel

    out_ref[...] = gram_dot(s[:, n:], s[:, n:])


def factor_and_invert(gram, normal):
    n = gram.shape[0]
    return pl.pallas_call(
        factor_kernel,
        out_shape=(jax.ShapeDtypeStruct((n, n), jnp.float32),) * 2,
        in_specs=[pl.BlockSpec(memory_space=pltpu.VMEM)] * 2,
        out_specs=(pl.BlockSpec(memory_space=pltpu.VMEM),) * 2,
        scratch_shapes=[
            pltpu.VMEM((n, n), jnp.float32),
            pltpu.VMEM((n, 2 * n), jnp.float32),
        ],
        compiler_params=pltpu.CompilerParams(vmem_limit_bytes=40 * 1024 * 1024),
        cost_estimate=pl.CostEstimate(
            flops=40 * n * n * n, bytes_accessed=20 * n * n, transcendentals=0
        ),
        name="factor_and_invert",
    )(gram, normal)


def local(snapshots, test_seeds, block_offsets):
    range_t, gram, normal, rhs = sketch(snapshots, test_seeds, block_offsets)
    rhs = lax.psum(rhs, "space")
    factor, inverse = factor_and_invert(gram, normal)
    weights = jnp.dot(inverse, rhs, precision=PRECISE)
    residual = snapshots - lax.dot_general(
        range_t, weights, (((0,), (0,)), ((), ())), precision=SPLIT
    )
    return (residual, factor)


def solution(mesh):
    return jax.shard_map(
        local,
        mesh=mesh,
        in_specs=(P("space", "tm"), P(), P()),
        out_specs=(P("space", "tm"), P()),
        check_vma=False,
    )
```

```python
import functools
import math
import types

import jax
import jax.numpy as jnp
from jax import lax
from jax.experimental import pallas as pl
from jax.experimental.pallas import tpu as pltpu
from jax.sharding import PartitionSpec as P

RANGE = 512
CORANGE = 1024
BLOCK = 64
TILE = 128
GROUP = 8
STRIP = 16
CHUNKS = 16
LAG = 2

MESH = pl.DeviceIdType.MESH
PRECISE = lax.Precision.HIGHEST
SPLIT = lax.Precision.HIGH


def scramble(values):
    values = jnp.bitwise_xor(values, lax.shift_right_logical(values, jnp.int32(16)))
    values = values * 73244475
    values = jnp.bitwise_xor(values, lax.shift_right_logical(values, jnp.int32(16)))
    values = values * 73244475
    values = jnp.bitwise_xor(values, lax.shift_right_logical(values, jnp.int32(16)))
    return values


def table_strip(row_hash, col_ids, scale):
    cell_hash = scramble(jnp.bitwise_xor(row_hash, col_ids * 374761393))
    total = None
    for stream in range(4):
        hashed = scramble(cell_hash + stream * 625341585) if stream else scramble(cell_hash)
        term = jnp.bitwise_and(hashed, 16777215)
        total = term if total is None else total + term
    return (total - 33554432).astype(jnp.float32) * jnp.float32(scale)


def halves(values):
    high = values.astype(jnp.bfloat16)
    low = (values - high.astype(jnp.float32)).astype(jnp.bfloat16)
    return high, low


def nt(left_side, right_side, precision=None):
    return lax.dot_general(
        left_side, right_side, (((1,), (1,)), ((), ())), precision=precision,
        preferred_element_type=jnp.float32,
    )


def nn(left_side, right_side):
    return jnp.dot(left_side, right_side, preferred_element_type=jnp.float32)


def gram_dot(left_side, right_side):
    return lax.dot_general(
        left_side, right_side, (((0,), (0,)), ((), ())), precision=PRECISE,
        preferred_element_type=jnp.float32,
    )


def dot(left_side, right_side):
    return jnp.dot(
        left_side, right_side, precision=PRECISE, preferred_element_type=jnp.float32
    )


def identity(size):
    rows = lax.broadcasted_iota(jnp.int32, (size, size), 0)
    cols = lax.broadcasted_iota(jnp.int32, (size, size), 1)
    return jnp.where(rows == cols, 1.0, 0.0).astype(jnp.float32)

def eliminate(blocks):
    size = blocks[0].shape[0]
    eye = identity(size)
    active = [jnp.concatenate([block, eye], axis=1) for block in blocks]
    width = 2 * size
    done = [[] for _ in blocks]
    for start in range(0, size, GROUP):
        rows = size - start
        row_id = lax.broadcasted_iota(jnp.int32, (rows, width), 0)
        columns = [
            [jnp.broadcast_to(work[:, start + j : start + j + 1], (rows, width)) for j in range(GROUP)]
            for work in active
        ]
        for j in range(GROUP):
            for place, column in enumerate(columns):
                work = active[place]
                below = jnp.where(row_id > j, column[j], 0.0)
                share = below * (1.0 / column[j][j : j + 1, :])
                for i in range(j + 1, GROUP):
                    column[i] = column[i] - share * column[i][j : j + 1, :]
                active[place] = work - share * work[j : j + 1, :]
        for place, work in enumerate(active):
            top = work[:GROUP]
            r = lax.broadcasted_iota(jnp.int32, (GROUP, width), 0) + start
            c = lax.broadcasted_iota(jnp.int32, (GROUP, width), 1)
            diagonal = jnp.sum(jnp.where(r == c, top, 0.0), axis=1, keepdims=True)
            done[place].append(top / jnp.sqrt(diagonal))
            active[place] = work[GROUP:]
    return [jnp.concatenate(rows, axis=0)[:, size:] for rows in done]

def panels(tiles):
    size = tiles[0].shape[0]
    works = [jnp.concatenate([tile, identity(size)], axis=1) for tile in tiles]
    done = [[] for _ in tiles]
    for lo in range(0, size, BLOCK):
        smalls = eliminate([work[:BLOCK, lo : lo + BLOCK] for work in works])
        for place, small in enumerate(smalls):
            rows = dot(small, works[place][:BLOCK])
            done[place].append(rows[:, size:])
            if lo + BLOCK < size:
                works[place] = works[place][BLOCK:] - gram_dot(rows[:, lo + BLOCK : size], rows)
    return [jnp.concatenate(rows, axis=0) for rows in done]


def factor_tile(base, g, s, inverse, factor):
    n = g.shape[0]
    end = base + TILE
    here = slice(base, end)
    g_inv, s_inv = panels([g[here, here], s[here, here]])
    g_panel = dot(g_inv, g[here, base:])
    rows = lax.broadcasted_iota(jnp.int32, (TILE, TILE), 0)
    cols = lax.broadcasted_iota(jnp.int32, (TILE, TILE), 1)
    factor[here, here] = jnp.where(cols >= rows, g_panel[:, :TILE], 0.0)
    inverse[here, here] = s_inv
    if base:
        factor[here, :base] = jnp.zeros((TILE, base), jnp.float32)
        before = dot(s_inv, inverse[here, :base])
        inverse[here, :base] = before
    if end < n:
        factor[here, end:] = g_panel[:, TILE:]
        s_panel = dot(s_inv, s[here, end:])
        g[end:, end:] -= gram_dot(g_panel[:, TILE:], g_panel[:, TILE:])
        s[end:, end:] -= gram_dot(s_panel, s_panel)
        if base:
            inverse[end:, :base] -= gram_dot(s_panel, before)
        inverse[end:, here] = -gram_dot(s_panel, s_inv)


class Shared:
    def __init__(self, place, block, slots, target, first, sems, core_sems):
        self.__dict__.update(vars(place))
        self.block, self.slots, self.target = block, slots, target
        self.sems, self.core_sems = sems, core_sems
        self.count = block.shape[0]
        self.rows = self.count // self.squares
        half = RANGE // 2 if core_sems is not None else 0
        self.mine = self.core * half + first
        self.theirs = (1 - self.core) * half + first
        self.sends = []

    def part(self, base, index):
        return pl.ds(pl.multiple_of(base + index * self.rows, 8), self.rows)

    def copy(self, stage, hop, source, target):
        device = (lax.rem(self.space + hop, self.squares), self.tm)
        return pltpu.make_async_remote_copy(
            src_ref=source, dst_ref=target, send_sem=self.sems.at[stage, 0, hop - 1],
            recv_sem=self.sems.at[stage, 1, hop - 1], device_id=device, device_id_type=MESH,
        )

    def scatter(self):
        for hop in range(1, self.squares):
            rows = self.part(0, lax.rem(self.space + hop, self.squares))
            copy = self.copy(0, hop, self.block.at[rows], self.slots.at[hop - 1])
            copy.start()
            self.sends.append(copy)

    def reduce(self):
        for copy in list(self.sends):
            copy.wait_recv()
        total = self.block[self.part(0, self.space), :]
        for hop in range(1, self.squares):
            total = total + self.slots[hop - 1]
        own = self.part(self.mine, self.space)
        self.target[own, :] = total
        self.gathers = []
        for hop in range(1, self.squares):
            copy = self.copy(1, hop, self.target.at[own], self.target.at[own])
            copy.start()
            self.gathers.append(copy)

    def collect(self):
        for hop in range(1, self.squares):
            rows = self.part(self.mine, lax.rem(self.space + self.squares - hop, self.squares))
            self.copy(1, hop, self.target.at[rows], self.target.at[rows]).wait_recv()
        self.pass_on = []
        if self.core_sems is not None:
            copy = core_copy(self, self.target, self.mine, self.count, self.core_sems)
            copy.start()
            self.pass_on.append(copy)

    def complete(self):
        core_copy(self, self.target, self.theirs, self.count, self.core_sems).wait_recv()

    def drain(self):
        for copy in self.sends + self.gathers + self.pass_on:
            copy.wait_send()


def core_copy(place, buffer, first, count, sems):
    rows = pl.ds(pl.multiple_of(first, 8), count)
    return pltpu.make_async_remote_copy(
        src_ref=buffer.at[rows], dst_ref=buffer.at[rows], send_sem=sems.at[0],
        recv_sem=sems.at[1], device_id=place.partner, device_id_type=MESH,
    )


def sketch_kernel(
    squares, line, seeds_ref, offsets_ref, a_ref, yt_out, factor_out, weights_out,
    a_hi, a_lo, o_hi, o_lo, p_hi, p_lo, give, got, own_range, yc, from_left, from_right, to_left,
    yt, mt, gt, m_block, m_slots, g_block, g_slots, w_hi, w_lo, normal, rhs,
    rhs_slots, rhs_sum, inverse, factor, weights,
    give_sems, line_sems, ycore_sems, m_sems, mcore_sems, g_sems, gcore_sems, r_sems, out_sems,
):
    space = lax.axis_index("space")
    tm = lax.axis_index("tm")
    core = lax.rem(tm, 2)
    z = lax.div(tm, 2)
    cells, snaps = a_ref.shape
    half_rows = RANGE // 2
    chunk = half_rows // CHUNKS
    groups, group_rows, _ = m_block.shape
    per_group = group_rows // chunk
    partner = (space, z * 2 + 1 - core)
    right = (space, lax.rem(z + 1, line) * 2 + core)
    left = (space, lax.rem(z + line - 1, line) * 2 + core)
    peers = [(lax.rem(space + index, squares), tm) for index in range(1, squares)]
    place = types.SimpleNamespace(
        space=space, tm=tm, core=core, squares=squares, partner=partner
    )

    barrier = pltpu.get_barrier_semaphore()
    for device in [partner, right, left] + peers:
        pl.semaphore_signal(barrier, inc=1, device_id=device, device_id_type=MESH)

    snap_ids = (
        offsets_ref[1] * (snaps * line * 2) + tm * snaps
        + lax.broadcasted_iota(jnp.int32, (1, snaps), 1)
    )
    snap_hash = scramble(snap_ids * 668265261 + seeds_ref[0])
    cell_ids = (
        offsets_ref[0] * (cells * squares) + space * cells
        + lax.broadcasted_iota(jnp.int32, (1, cells), 1)
    )
    cell_hash = scramble(cell_ids * 668265261 + seeds_ref[1])
    omega_scale = math.sqrt(3.0) / 16777216.0 / math.sqrt(cells * squares * snaps * line * 2)
    psi_scale = math.sqrt(3.0) / 16777216.0 / math.sqrt(cells * squares)

    @pl.loop(0, cells // 128)
    def _(index):
        rows = pl.ds(pl.multiple_of(index * 128, 128), 128)
        a_hi[rows, :], a_lo[rows, :] = halves(a_ref[rows, :])

    half_range = half_rows // 2

    def range_part(target, owner, turn):
        offset = turn * half_range

        @pl.loop(0, half_range // STRIP)
        def _(index):
            base = pl.multiple_of(index * STRIP, STRIP)
            ids = lax.broadcasted_iota(jnp.int32, (STRIP, snaps), 0) + (
                owner * half_rows + offset + base
            )
            strip = table_strip(snap_hash, ids, omega_scale)
            o_hi[pl.ds(base, STRIP), :], o_lo[pl.ds(base, STRIP), :] = halves(strip)

        @pl.loop(0, cells // 512)
        def _(index):
            here = pl.ds(pl.multiple_of(index * 512, 512), 512)
            target[offset : offset + half_range, here] = (
                nt(o_hi[...], a_hi[here, :]) + nt(o_hi[...], a_lo[here, :])
                + nt(o_lo[...], a_hi[here, :])
            )

    def psi(lo, hi):
        @pl.loop(lo // STRIP, hi // STRIP)
        def _(index):
            base = pl.multiple_of(index * STRIP, STRIP)
            ids = lax.broadcasted_iota(jnp.int32, (STRIP, cells), 0) + base
            strip = table_strip(cell_hash, ids, psi_scale)
            p_hi[pl.ds(base, STRIP), :], p_lo[pl.ds(base, STRIP), :] = halves(strip)

    def line_copy(way, index, source):
        target = from_left if way == 0 else from_right
        return pltpu.make_async_remote_copy(
            src_ref=source, dst_ref=target.at[index], send_sem=line_sems.at[way, 0, index],
            recv_sem=line_sems.at[way, 1, index],
            device_id=right if way == 0 else left, device_id_type=MESH,
        )

    gives = []
    per_turn = CHUNKS // 2
    for turn in range(2):
        range_part(give, 1 - core, turn)
        if turn == 0:
            pl.semaphore_wait(barrier, 3 + len(peers))
        rows = pl.ds(turn * half_range, half_range)
        copy = pltpu.make_async_remote_copy(
            src_ref=give.at[rows], dst_ref=got.at[rows], send_sem=give_sems.at[0, turn],
            recv_sem=give_sems.at[1, turn], device_id=partner, device_id_type=MESH,
        )
        copy.start()
        gives.append(copy)
        range_part(own_range, core, turn)
        copy.wait_recv()
        for index in range(turn * per_turn, (turn + 1) * per_turn):
            rows = pl.ds(index * chunk, chunk)
            yc[index] = own_range[rows, :] + got[rows, :]

            @pl.when(z == 0)
            def _():
                line_copy(0, index, yc.at[index]).start()

            @pl.when(z == line - 1)
            def _():
                line_copy(1, index, yc.at[index]).start()

    def line_step(step):
        index = step - 1 - LAG * (z - 1)

        @pl.when((z > 0) & (index >= 0) & (index < CHUNKS))
        def _():
            line_copy(0, index, yc.at[index]).wait_recv()
            from_left[index] = from_left[index] + yc[index]

            @pl.when(z < line - 1)
            def _():
                line_copy(0, index, from_left.at[index]).start()

        other = step - 1 - LAG * (line - 2 - z)

        @pl.when((z < line - 1) & (other >= 0) & (other < CHUNKS))
        def _():
            line_copy(1, other, yc.at[other]).wait_recv()

            @pl.when(z > 0)
            def _():
                to_left[other] = from_right[other] + yc[other]
                line_copy(1, other, to_left.at[other]).start()

        done = step - 1 - LAG * (line - 2)
        if 0 <= done < CHUNKS:
            rows = pl.ds(pl.multiple_of(core * half_rows + done * chunk, 8), chunk)

            @pl.when(z == 0)
            def _():
                yt[rows, :] = yc[done] + from_right[done]

            @pl.when(z == line - 1)
            def _():
                yt[rows, :] = from_left[done]

            @pl.when((z > 0) & (z < line - 1))
            def _():
                yt[rows, :] = from_left[done] + from_right[done]

    def line_drain():
        @pl.when(z < line - 1)
        def _():
            for index in range(CHUNKS):
                line_copy(0, index, yc.at[index]).wait_send()

        @pl.when(z > 0)
        def _():
            for index in range(CHUNKS):
                line_copy(1, index, yc.at[index]).wait_send()

    def corange(lo, hi):
        for start in range(lo, hi, 256):
            here = pl.ds(start, 256)
            part = (
                nn(p_hi[here, :], a_hi[...]) + nn(p_hi[here, :], a_lo[...])
                + nn(p_lo[here, :], a_hi[...])
            )
            w_hi[here, :], w_lo[here, :] = halves(part)

    y_pass, shared = [], []

    def couple(group):
        first = group * group_rows
        copy = core_copy(place, yt, core * half_rows + first, group_rows, ycore_sems.at[group])
        copy.start()
        y_pass.append(copy)
        rows = pl.ds(pl.multiple_of(core * half_rows + first, 8), group_rows)
        high, low = halves(yt[rows, :])
        both = jnp.concatenate([high, low], axis=0)
        for tile in range(CORANGE // 256):
            here = pl.ds(tile * 256, 256)
            most = nt(both, p_hi[here, :])
            m_block[group, :, here] = (
                most[:group_rows] + most[group_rows:] + nt(high, p_lo[here, :])
            )
        total = Shared(
            place, m_block.at[group], m_slots.at[group], mt, first, m_sems.at[group],
            mcore_sems.at[group],
        )
        total.scatter()
        shared.append(total)

    steps = list(range(1, CHUNKS + 1 + LAG * (line - 2)))
    strips = CORANGE // 8
    for turn in range(8):
        psi(turn * strips, (turn + 1) * strips)
        if turn >= 1:
            line_step(steps.pop(0))
    for group in range(groups):
        last = (group + 1) * per_group + LAG * (line - 2)
        while steps and steps[0] <= last:
            line_step(steps.pop(0))
        couple(group)
        if group >= 1:
            shared[group - 1].reduce()
        if group >= 2:
            shared[group - 2].collect()
        if group < groups - 1:
            corange(CORANGE // groups * group, CORANGE // groups * (group + 1))
    for group in range(groups):
        rows = (1 - core) * half_rows + group * group_rows
        core_copy(place, yt, rows, group_rows, ycore_sems.at[group]).wait_recv()
    y_store = pltpu.make_async_copy(yt, yt_out, out_sems.at[0])
    y_store.start()
    shared[groups - 2].collect()
    corange(CORANGE // groups * (groups - 1), CORANGE)
    shared[groups - 1].reduce()
    mine = pl.ds(pl.multiple_of(core * half_rows, 8), half_rows)
    g_block[...] = nt(yt[mine, :], yt[...], PRECISE)
    g_shared = Shared(place, g_block, g_slots, gt, 0, g_sems, gcore_sems)
    g_shared.scatter()
    shared[groups - 1].collect()
    for total in shared:
        total.complete()

    def right_side(lo):
        here = pl.ds(lo, 256)
        m_hi, m_lo = halves(mt[here, :])
        rhs[here, :] = nn(m_hi, w_hi[...]) + nn(m_hi, w_lo[...]) + nn(m_lo, w_hi[...])

    for lo in range(0, RANGE, 256):
        right_side(lo)
    g_shared.reduce()
    for lo in range(0, RANGE, 256):
        normal[lo : lo + 256, lo:] = nt(mt[lo : lo + 256, :], mt[lo:, :], PRECISE)
    g_shared.collect()
    r_shared = Shared(place, rhs, rhs_slots, rhs_sum, 0, r_sems, None)
    r_shared.scatter()
    g_shared.complete()
    g_shared.drain()

    for base in range(0, RANGE, TILE):
        factor_tile(base, gt, normal, inverse, factor)
        if base == 0:
            r_shared.reduce()
    f_store = pltpu.make_async_copy(factor, factor_out, out_sems.at[1])
    f_store.start()
    r_shared.collect()
    for base in range(0, RANGE, TILE):
        here, end = slice(base, base + TILE), base + TILE
        solved = dot(inverse[here, :end], rhs_sum[:end, :])
        part = gram_dot(inverse[here, :end], solved)
        if base:
            weights[:base, :] += part[:base]
        weights[here, :] = part[base:]
    w_store = pltpu.make_async_copy(weights, weights_out, out_sems.at[2])
    w_store.start()

    for copy in gives + y_pass:
        copy.wait_send()
    for total in shared + [r_shared]:
        total.drain()
    line_drain()
    for copy in (y_store, f_store, w_store):
        copy.wait()


def sketch(snapshots, test_seeds, block_offsets):
    cells, snaps = snapshots.shape
    squares = lax.axis_size("space")
    line = lax.axis_size("tm") // 2
    half_rows = RANGE // 2
    chunk = half_rows // CHUNKS
    group_rows = max(half_rows // 4, 8 * squares)
    groups = half_rows // group_rows
    f32, bf16 = jnp.float32, jnp.bfloat16
    dma = pltpu.SemaphoreType.DMA
    scratch = [
        pltpu.VMEM((cells, snaps), bf16), pltpu.VMEM((cells, snaps), bf16),
        pltpu.VMEM((half_rows // 2, snaps), bf16), pltpu.VMEM((half_rows // 2, snaps), bf16),
        pltpu.VMEM((CORANGE, cells), bf16), pltpu.VMEM((CORANGE, cells), bf16),
        pltpu.VMEM((half_rows, cells), f32), pltpu.VMEM((half_rows, cells), f32),
        pltpu.VMEM((half_rows, cells), f32),
        pltpu.VMEM((CHUNKS, chunk, cells), f32), pltpu.VMEM((CHUNKS, chunk, cells), f32),
        pltpu.VMEM((CHUNKS, chunk, cells), f32), pltpu.VMEM((CHUNKS, chunk, cells), f32),
        pltpu.VMEM((RANGE, cells), f32), pltpu.VMEM((RANGE, CORANGE), f32),
        pltpu.VMEM((RANGE, RANGE), f32),
        pltpu.VMEM((groups, group_rows, CORANGE), f32),
        pltpu.VMEM((groups, squares - 1, group_rows // squares, CORANGE), f32),
        pltpu.VMEM((half_rows, RANGE), f32),
        pltpu.VMEM((squares - 1, half_rows // squares, RANGE), f32),
        pltpu.VMEM((CORANGE, snaps), bf16), pltpu.VMEM((CORANGE, snaps), bf16),
        pltpu.VMEM((RANGE, RANGE), f32), pltpu.VMEM((RANGE, snaps), f32),
        pltpu.VMEM((squares - 1, RANGE // squares, snaps), f32), pltpu.VMEM((RANGE, snaps), f32),
        pltpu.VMEM((RANGE, RANGE), f32), pltpu.VMEM((RANGE, RANGE), f32),
        pltpu.VMEM((RANGE, snaps), f32),
        dma((2, 2)), dma((2, 2, CHUNKS)), dma((groups, 2)),
        dma((groups, 2, 2, squares - 1)), dma((groups, 2)),
        dma((2, 2, squares - 1)), dma((2,)), dma((2, 2, squares - 1)), dma((3,)),
    ]
    flops = 2 * 3 * cells * snaps * (RANGE + CORANGE) + 2 * 9 * RANGE * RANGE * CORANGE
    return pl.pallas_call(
        functools.partial(sketch_kernel, squares, line),
        out_shape=(
            jax.ShapeDtypeStruct((RANGE, cells), f32),
            jax.ShapeDtypeStruct((RANGE, RANGE), f32),
            jax.ShapeDtypeStruct((RANGE, snaps), f32),
        ),
        in_specs=[
            pl.BlockSpec(memory_space=pltpu.SMEM), pl.BlockSpec(memory_space=pltpu.SMEM),
            pl.BlockSpec(memory_space=pltpu.VMEM),
        ],
        out_specs=(pl.BlockSpec(memory_space=pl.ANY),) * 3,
        scratch_shapes=scratch,
        compiler_params=pltpu.CompilerParams(
            collective_id=0, has_side_effects=True, vmem_limit_bytes=52 * 1024 * 1024
        ),
        cost_estimate=pl.CostEstimate(
            flops=flops, bytes_accessed=8 * cells * snaps, transcendentals=0
        ),
        name="sketch",
    )(test_seeds, block_offsets, snapshots)


def local(snapshots, test_seeds, block_offsets):
    range_t, factor, weights = sketch(snapshots, test_seeds, block_offsets)
    residual = snapshots - lax.dot_general(
        range_t, weights, (((0,), (0,)), ((), ())), precision=SPLIT
    )
    return (residual, factor)


def solution(mesh):
    return jax.shard_map(
        local,
        mesh=mesh,
        in_specs=(P("space", "tm"), P(), P()),
        out_specs=(P("space", "tm"), P()),
        check_vma=False,
    )
```

```python
import functools
import math
import types

import jax
import jax.numpy as jnp
from jax import lax
from jax.experimental import pallas as pl
from jax.experimental.pallas import tpu as pltpu
from jax.sharding import PartitionSpec as P

RANGE = 512
CORANGE = 1024
BLOCK = 64
TILE = 128
GROUP = 8
STRIP = 16
CHUNKS = 16
LAG = 3

MESH = pl.DeviceIdType.MESH
PRECISE = lax.Precision.HIGHEST
SPLIT = lax.Precision.HIGH


def scramble(values):
    values = jnp.bitwise_xor(values, lax.shift_right_logical(values, jnp.int32(16)))
    values = values * 73244475
    values = jnp.bitwise_xor(values, lax.shift_right_logical(values, jnp.int32(16)))
    values = values * 73244475
    values = jnp.bitwise_xor(values, lax.shift_right_logical(values, jnp.int32(16)))
    return values


def table_strip(row_hash, col_ids, scale):
    cell_hash = scramble(jnp.bitwise_xor(row_hash, col_ids * 374761393))
    total = None
    for stream in range(4):
        hashed = scramble(cell_hash + stream * 625341585) if stream else scramble(cell_hash)
        term = jnp.bitwise_and(hashed, 16777215)
        total = term if total is None else total + term
    return (total - 33554432).astype(jnp.float32) * jnp.float32(scale)


def halves(values):
    high = values.astype(jnp.bfloat16)
    low = (values - high.astype(jnp.float32)).astype(jnp.bfloat16)
    return high, low


def nt(left_side, right_side, precision=None):
    return lax.dot_general(
        left_side, right_side, (((1,), (1,)), ((), ())), precision=precision,
        preferred_element_type=jnp.float32,
    )


def nn(left_side, right_side):
    return jnp.dot(left_side, right_side, preferred_element_type=jnp.float32)


def gram_dot(left_side, right_side):
    return lax.dot_general(
        left_side, right_side, (((0,), (0,)), ((), ())), precision=PRECISE,
        preferred_element_type=jnp.float32,
    )


def dot(left_side, right_side):
    return jnp.dot(
        left_side, right_side, precision=PRECISE, preferred_element_type=jnp.float32
    )


def identity(size):
    rows = lax.broadcasted_iota(jnp.int32, (size, size), 0)
    cols = lax.broadcasted_iota(jnp.int32, (size, size), 1)
    return jnp.where(rows == cols, 1.0, 0.0).astype(jnp.float32)

def eliminate(blocks):
    size = blocks[0].shape[0]
    eye = identity(size)
    active = [jnp.concatenate([block, eye], axis=1) for block in blocks]
    width = 2 * size
    done = [[] for _ in blocks]
    for start in range(0, size, GROUP):
        rows = size - start
        row_id = lax.broadcasted_iota(jnp.int32, (rows, width), 0)
        columns = [
            [jnp.broadcast_to(work[:, start + j : start + j + 1], (rows, width)) for j in range(GROUP)]
            for work in active
        ]
        for j in range(GROUP):
            for place, column in enumerate(columns):
                work = active[place]
                below = jnp.where(row_id > j, column[j], 0.0)
                share = below * (1.0 / column[j][j : j + 1, :])
                for i in range(j + 1, GROUP):
                    column[i] = column[i] - share * column[i][j : j + 1, :]
                active[place] = work - share * work[j : j + 1, :]
        for place, work in enumerate(active):
            top = work[:GROUP]
            r = lax.broadcasted_iota(jnp.int32, (GROUP, width), 0) + start
            c = lax.broadcasted_iota(jnp.int32, (GROUP, width), 1)
            diagonal = jnp.sum(jnp.where(r == c, top, 0.0), axis=1, keepdims=True)
            done[place].append(top / jnp.sqrt(diagonal))
            active[place] = work[GROUP:]
    return [jnp.concatenate(rows, axis=0)[:, size:] for rows in done]

def panels(tiles):
    size = tiles[0].shape[0]
    works = [jnp.concatenate([tile, identity(size)], axis=1) for tile in tiles]
    done = [[] for _ in tiles]
    for lo in range(0, size, BLOCK):
        smalls = eliminate([work[:BLOCK, lo : lo + BLOCK] for work in works])
        for place, small in enumerate(smalls):
            rows = dot(small, works[place][:BLOCK])
            done[place].append(rows[:, size:])
            if lo + BLOCK < size:
                works[place] = works[place][BLOCK:] - gram_dot(rows[:, lo + BLOCK : size], rows)
    return [jnp.concatenate(rows, axis=0) for rows in done]


def factor_tile(base, g, s, inverse, factor):
    n = g.shape[0]
    end = base + TILE
    here = slice(base, end)
    g_inv, s_inv = panels([g[here, here], s[here, here]])
    g_panel = dot(g_inv, g[here, base:])
    rows = lax.broadcasted_iota(jnp.int32, (TILE, TILE), 0)
    cols = lax.broadcasted_iota(jnp.int32, (TILE, TILE), 1)
    factor[here, here] = jnp.where(cols >= rows, g_panel[:, :TILE], 0.0)
    inverse[here, here] = s_inv
    if base:
        factor[here, :base] = jnp.zeros((TILE, base), jnp.float32)
        before = dot(s_inv, inverse[here, :base])
        inverse[here, :base] = before
    if end < n:
        factor[here, end:] = g_panel[:, TILE:]
        s_panel = dot(s_inv, s[here, end:])
        g[end:, end:] -= gram_dot(g_panel[:, TILE:], g_panel[:, TILE:])
        s[end:, end:] -= gram_dot(s_panel, s_panel)
        if base:
            inverse[end:, :base] -= gram_dot(s_panel, before)
        inverse[end:, here] = -gram_dot(s_panel, s_inv)


class Shared:
    def __init__(self, place, block, slots, target, first, sems, core_sems):
        self.__dict__.update(vars(place))
        self.block, self.slots, self.target = block, slots, target
        self.sems, self.core_sems = sems, core_sems
        self.count = block.shape[0]
        self.rows = self.count // self.squares
        half = RANGE // 2 if core_sems is not None else 0
        self.mine = self.core * half + first
        self.theirs = (1 - self.core) * half + first
        self.sends = []

    def part(self, base, index):
        return pl.ds(pl.multiple_of(base + index * self.rows, 8), self.rows)

    def copy(self, stage, hop, source, target):
        device = (lax.rem(self.space + hop, self.squares), self.tm)
        return pltpu.make_async_remote_copy(
            src_ref=source, dst_ref=target, send_sem=self.sems.at[stage, 0, hop - 1],
            recv_sem=self.sems.at[stage, 1, hop - 1], device_id=device, device_id_type=MESH,
        )

    def scatter(self):
        for hop in range(1, self.squares):
            rows = self.part(0, lax.rem(self.space + hop, self.squares))
            copy = self.copy(0, hop, self.block.at[rows], self.slots.at[hop - 1])
            copy.start()
            self.sends.append(copy)

    def reduce(self):
        for copy in list(self.sends):
            copy.wait_recv()
        total = self.block[self.part(0, self.space), :]
        for hop in range(1, self.squares):
            total = total + self.slots[hop - 1]
        own = self.part(self.mine, self.space)
        self.target[own, :] = total
        self.gathers = []
        for hop in range(1, self.squares):
            copy = self.copy(1, hop, self.target.at[own], self.target.at[own])
            copy.start()
            self.gathers.append(copy)

    def collect(self):
        for hop in range(1, self.squares):
            rows = self.part(self.mine, lax.rem(self.space + self.squares - hop, self.squares))
            self.copy(1, hop, self.target.at[rows], self.target.at[rows]).wait_recv()
        self.pass_on = []
        if self.core_sems is not None:
            copy = core_copy(self, self.target, self.mine, self.count, self.core_sems)
            copy.start()
            self.pass_on.append(copy)

    def complete(self):
        core_copy(self, self.target, self.theirs, self.count, self.core_sems).wait_recv()

    def drain(self):
        for copy in self.sends + self.gathers + self.pass_on:
            copy.wait_send()


def core_copy(place, buffer, first, count, sems):
    rows = pl.ds(pl.multiple_of(first, 8), count)
    return pltpu.make_async_remote_copy(
        src_ref=buffer.at[rows], dst_ref=buffer.at[rows], send_sem=sems.at[0],
        recv_sem=sems.at[1], device_id=place.partner, device_id_type=MESH,
    )


def sketch_kernel(
    squares, line, seeds_ref, offsets_ref, a_in, yh_out, yl_out, factor_out, wh_out, wl_out,
    a_ref, a_hi, a_lo, o_hi, o_lo, p_hi, p_lo, give, got, own_range, yc, from_left, from_right, to_left,
    yt, mt, gt, m_block, m_slots, g_block, g_slots, w_hi, w_lo, normal, rhs,
    rhs_slots, rhs_sum, inverse, factor, weights, y_hi, y_lo, wt_hi, wt_lo,
    give_sems, line_sems, ycore_sems, m_sems, mcore_sems, g_sems, gcore_sems, r_sems, out_sems,
):
    space = lax.axis_index("space")
    tm = lax.axis_index("tm")
    core = lax.rem(tm, 2)
    z = lax.div(tm, 2)
    cells, snaps = a_ref.shape
    half_rows = RANGE // 2
    chunk = half_rows // CHUNKS
    groups, group_rows, _ = m_block.shape
    per_group = group_rows // chunk
    partner = (space, z * 2 + 1 - core)
    right = (space, lax.rem(z + 1, line) * 2 + core)
    left = (space, lax.rem(z + line - 1, line) * 2 + core)
    peers = [(lax.rem(space + index, squares), tm) for index in range(1, squares)]
    place = types.SimpleNamespace(
        space=space, tm=tm, core=core, squares=squares, partner=partner
    )

    a_load = pltpu.make_async_copy(a_in, a_ref, out_sems.at[5])
    a_load.start()
    barrier = pltpu.get_barrier_semaphore()
    for device in [partner, right, left] + peers:
        pl.semaphore_signal(barrier, inc=1, device_id=device, device_id_type=MESH)

    snap_ids = (
        offsets_ref[1] * (snaps * line * 2) + tm * snaps
        + lax.broadcasted_iota(jnp.int32, (1, snaps), 1)
    )
    snap_hash = scramble(snap_ids * 668265261 + seeds_ref[0])
    cell_ids = (
        offsets_ref[0] * (cells * squares) + space * cells
        + lax.broadcasted_iota(jnp.int32, (1, cells), 1)
    )
    cell_hash = scramble(cell_ids * 668265261 + seeds_ref[1])
    omega_scale = math.sqrt(3.0) / 16777216.0 / math.sqrt(cells * squares * snaps * line * 2)
    psi_scale = math.sqrt(3.0) / 16777216.0 / math.sqrt(cells * squares)

    def split_snapshots():
        a_load.wait()

        @pl.loop(0, cells // 128)
        def _(index):
            rows = pl.ds(pl.multiple_of(index * 128, 128), 128)
            a_hi[rows, :], a_lo[rows, :] = halves(a_ref[rows, :])

    half_range = half_rows // 2

    def omega(owner, turn):
        offset = turn * half_range

        @pl.loop(0, half_range // STRIP)
        def _(index):
            base = pl.multiple_of(index * STRIP, STRIP)
            ids = lax.broadcasted_iota(jnp.int32, (STRIP, snaps), 0) + (
                owner * half_rows + offset + base
            )
            strip = table_strip(snap_hash, ids, omega_scale)
            o_hi[pl.ds(base, STRIP), :], o_lo[pl.ds(base, STRIP), :] = halves(strip)

    def range_part(target, turn):
        offset = turn * half_range

        @pl.loop(0, cells // 512)
        def _(index):
            here = pl.ds(pl.multiple_of(index * 512, 512), 512)
            target[offset : offset + half_range, here] = (
                nt(o_hi[...], a_hi[here, :]) + nt(o_hi[...], a_lo[here, :])
                + nt(o_lo[...], a_hi[here, :])
            )

    def psi(lo, hi):
        @pl.loop(lo // STRIP, hi // STRIP)
        def _(index):
            base = pl.multiple_of(index * STRIP, STRIP)
            ids = lax.broadcasted_iota(jnp.int32, (STRIP, cells), 0) + base
            strip = table_strip(cell_hash, ids, psi_scale)
            p_hi[pl.ds(base, STRIP), :], p_lo[pl.ds(base, STRIP), :] = halves(strip)

    def line_copy(way, index, source):
        target = from_left if way == 0 else from_right
        return pltpu.make_async_remote_copy(
            src_ref=source, dst_ref=target.at[index], send_sem=line_sems.at[way, 0, index],
            recv_sem=line_sems.at[way, 1, index],
            device_id=right if way == 0 else left, device_id_type=MESH,
        )

    gives = []
    per_turn = CHUNKS // 2
    for turn in range(2):
        omega(1 - core, turn)
        if turn == 0:
            split_snapshots()
        range_part(give, turn)
        if turn == 0:
            pl.semaphore_wait(barrier, 3 + len(peers))
        rows = pl.ds(turn * half_range, half_range)
        copy = pltpu.make_async_remote_copy(
            src_ref=give.at[rows], dst_ref=got.at[rows], send_sem=give_sems.at[0, turn],
            recv_sem=give_sems.at[1, turn], device_id=partner, device_id_type=MESH,
        )
        copy.start()
        gives.append(copy)
        omega(core, turn)
        range_part(own_range, turn)
        copy.wait_recv()
        for index in range(turn * per_turn, (turn + 1) * per_turn):
            rows = pl.ds(index * chunk, chunk)
            yc[index] = own_range[rows, :] + got[rows, :]

            @pl.when(z == 0)
            def _():
                line_copy(0, index, yc.at[index]).start()

            @pl.when(z == line - 1)
            def _():
                line_copy(1, index, yc.at[index]).start()

    def line_step(step):
        index = step - 1 - LAG * (z - 1)

        @pl.when((z > 0) & (index >= 0) & (index < CHUNKS))
        def _():
            line_copy(0, index, yc.at[index]).wait_recv()
            from_left[index] = from_left[index] + yc[index]

            @pl.when(z < line - 1)
            def _():
                line_copy(0, index, from_left.at[index]).start()

        other = step - 1 - LAG * (line - 2 - z)

        @pl.when((z < line - 1) & (other >= 0) & (other < CHUNKS))
        def _():
            line_copy(1, other, yc.at[other]).wait_recv()

            @pl.when(z > 0)
            def _():
                to_left[other] = from_right[other] + yc[other]
                line_copy(1, other, to_left.at[other]).start()

        done = step - 1 - LAG * (line - 2)
        if 0 <= done < CHUNKS:
            rows = pl.ds(pl.multiple_of(core * half_rows + done * chunk, 8), chunk)

            @pl.when(z == 0)
            def _():
                yt[rows, :] = yc[done] + from_right[done]

            @pl.when(z == line - 1)
            def _():
                yt[rows, :] = from_left[done]

            @pl.when((z > 0) & (z < line - 1))
            def _():
                yt[rows, :] = from_left[done] + from_right[done]

    def line_drain():
        @pl.when(z < line - 1)
        def _():
            for index in range(CHUNKS):
                line_copy(0, index, yc.at[index]).wait_send()

        @pl.when(z > 0)
        def _():
            for index in range(CHUNKS):
                line_copy(1, index, yc.at[index]).wait_send()

    def corange(lo, hi):
        for start in range(lo, hi, 256):
            here = pl.ds(start, 256)
            part = (
                nn(p_hi[here, :], a_hi[...]) + nn(p_hi[here, :], a_lo[...])
                + nn(p_lo[here, :], a_hi[...])
            )
            w_hi[here, :], w_lo[here, :] = halves(part)

    y_pass, shared = [], []

    def couple(group):
        first = group * group_rows
        copy = core_copy(place, yt, core * half_rows + first, group_rows, ycore_sems.at[group])
        copy.start()
        y_pass.append(copy)
        rows = pl.ds(pl.multiple_of(core * half_rows + first, 8), group_rows)
        high, low = halves(yt[rows, :])
        both = jnp.concatenate([high, low], axis=0)
        for tile in range(CORANGE // 256):
            here = pl.ds(tile * 256, 256)
            most = nt(both, p_hi[here, :])
            m_block[group, :, here] = (
                most[:group_rows] + most[group_rows:] + nt(high, p_lo[here, :])
            )
        total = Shared(
            place, m_block.at[group], m_slots.at[group], mt, first, m_sems.at[group],
            mcore_sems.at[group],
        )
        total.scatter()
        shared.append(total)

    steps = list(range(1, CHUNKS + 1 + LAG * (line - 2)))
    strips = CORANGE // 8
    for turn in range(8):
        psi(turn * strips, (turn + 1) * strips)
        if turn >= 1:
            line_step(steps.pop(0))
    for group in range(groups):
        last = (group + 1) * per_group + LAG * (line - 2)
        while steps and steps[0] <= last:
            line_step(steps.pop(0))
        couple(group)
        if group >= 1:
            shared[group - 1].reduce()
        if group >= 2:
            shared[group - 2].collect()
        if group < groups - 1:
            corange(CORANGE // groups * group, CORANGE // groups * (group + 1))
    for group in range(groups):
        rows = (1 - core) * half_rows + group * group_rows
        core_copy(place, yt, rows, group_rows, ycore_sems.at[group]).wait_recv()
    mine = pl.ds(pl.multiple_of(core * half_rows, 8), half_rows)
    g_block[...] = nt(yt[mine, :], yt[...], PRECISE)
    g_shared = Shared(place, g_block, g_slots, gt, 0, g_sems, gcore_sems)
    g_shared.scatter()
    corange(CORANGE // groups * (groups - 1), CORANGE)
    shared[groups - 1].reduce()

    @pl.loop(0, cells // 128)
    def _(index):
        here = pl.ds(pl.multiple_of(index * 128, 128), 128)
        y_hi[here, :], y_lo[here, :] = halves(jnp.transpose(yt[:, here]))

    stores = [
        pltpu.make_async_copy(y_hi, yh_out, out_sems.at[0]),
        pltpu.make_async_copy(y_lo, yl_out, out_sems.at[1]),
    ]
    for copy in stores:
        copy.start()
    shared[groups - 2].collect()
    g_shared.reduce()
    shared[groups - 1].collect()
    for total in shared:
        total.complete()
    for lo in range(0, RANGE, 256):
        normal[lo : lo + 256, lo:] = nt(mt[lo : lo + 256, :], mt[lo:, :], PRECISE)
    g_shared.collect()

    def right_side(lo):
        here = pl.ds(lo, 256)
        m_hi, m_lo = halves(mt[here, :])
        rhs[here, :] = nn(m_hi, w_hi[...]) + nn(m_hi, w_lo[...]) + nn(m_lo, w_hi[...])

    for lo in range(0, RANGE, 256):
        right_side(lo)
    r_shared = Shared(place, rhs, rhs_slots, rhs_sum, 0, r_sems, None)
    r_shared.scatter()
    g_shared.complete()
    g_shared.drain()

    for base in range(0, RANGE, TILE):
        factor_tile(base, gt, normal, inverse, factor)
        if base == 0:
            r_shared.reduce()
    stores.append(pltpu.make_async_copy(factor, factor_out, out_sems.at[2]))
    stores[-1].start()
    r_shared.collect()
    for base in range(0, RANGE, TILE):
        here, end = slice(base, base + TILE), base + TILE
        solved = dot(inverse[here, :end], rhs_sum[:end, :])
        part = gram_dot(inverse[here, :end], solved)
        if base:
            weights[:base, :] += part[:base]
        weights[here, :] = part[base:]
    wt_hi[...], wt_lo[...] = halves(weights[...])
    for source, target, sem in ((wt_hi, wh_out, 3), (wt_lo, wl_out, 4)):
        stores.append(pltpu.make_async_copy(source, target, out_sems.at[sem]))
        stores[-1].start()

    for copy in gives + y_pass:
        copy.wait_send()
    for total in shared + [r_shared]:
        total.drain()
    line_drain()
    for copy in stores:
        copy.wait()


def sketch(snapshots, test_seeds, block_offsets):
    cells, snaps = snapshots.shape
    squares = lax.axis_size("space")
    line = lax.axis_size("tm") // 2
    half_rows = RANGE // 2
    chunk = half_rows // CHUNKS
    group_rows = max(half_rows // 4, 8 * squares)
    groups = half_rows // group_rows
    f32, bf16 = jnp.float32, jnp.bfloat16
    dma = pltpu.SemaphoreType.DMA
    scratch = [
        pltpu.VMEM((cells, snaps), f32),
        pltpu.VMEM((cells, snaps), bf16), pltpu.VMEM((cells, snaps), bf16),
        pltpu.VMEM((half_rows // 2, snaps), bf16), pltpu.VMEM((half_rows // 2, snaps), bf16),
        pltpu.VMEM((CORANGE, cells), bf16), pltpu.VMEM((CORANGE, cells), bf16),
        pltpu.VMEM((half_rows, cells), f32), pltpu.VMEM((half_rows, cells), f32),
        pltpu.VMEM((half_rows, cells), f32),
        pltpu.VMEM((CHUNKS, chunk, cells), f32), pltpu.VMEM((CHUNKS, chunk, cells), f32),
        pltpu.VMEM((CHUNKS, chunk, cells), f32), pltpu.VMEM((CHUNKS, chunk, cells), f32),
        pltpu.VMEM((RANGE, cells), f32), pltpu.VMEM((RANGE, CORANGE), f32),
        pltpu.VMEM((RANGE, RANGE), f32),
        pltpu.VMEM((groups, group_rows, CORANGE), f32),
        pltpu.VMEM((groups, squares - 1, group_rows // squares, CORANGE), f32),
        pltpu.VMEM((half_rows, RANGE), f32),
        pltpu.VMEM((squares - 1, half_rows // squares, RANGE), f32),
        pltpu.VMEM((CORANGE, snaps), bf16), pltpu.VMEM((CORANGE, snaps), bf16),
        pltpu.VMEM((RANGE, RANGE), f32), pltpu.VMEM((RANGE, snaps), f32),
        pltpu.VMEM((squares - 1, RANGE // squares, snaps), f32), pltpu.VMEM((RANGE, snaps), f32),
        pltpu.VMEM((RANGE, RANGE), f32), pltpu.VMEM((RANGE, RANGE), f32),
        pltpu.VMEM((RANGE, snaps), f32),
        pltpu.VMEM((cells, RANGE), bf16), pltpu.VMEM((cells, RANGE), bf16),
        pltpu.VMEM((RANGE, snaps), bf16), pltpu.VMEM((RANGE, snaps), bf16),
        dma((2, 2)), dma((2, 2, CHUNKS)), dma((groups, 2)),
        dma((groups, 2, 2, squares - 1)), dma((groups, 2)),
        dma((2, 2, squares - 1)), dma((2,)), dma((2, 2, squares - 1)), dma((6,)),
    ]
    flops = 2 * 3 * cells * snaps * (RANGE + CORANGE) + 2 * 9 * RANGE * RANGE * CORANGE
    return pl.pallas_call(
        functools.partial(sketch_kernel, squares, line),
        out_shape=(
            jax.ShapeDtypeStruct((cells, RANGE), bf16),
            jax.ShapeDtypeStruct((cells, RANGE), bf16),
            jax.ShapeDtypeStruct((RANGE, RANGE), f32),
            jax.ShapeDtypeStruct((RANGE, snaps), bf16),
            jax.ShapeDtypeStruct((RANGE, snaps), bf16),
        ),
        in_specs=[
            pl.BlockSpec(memory_space=pltpu.SMEM), pl.BlockSpec(memory_space=pltpu.SMEM),
            pl.BlockSpec(memory_space=pl.ANY),
        ],
        out_specs=(pl.BlockSpec(memory_space=pl.ANY),) * 5,
        scratch_shapes=scratch,
        compiler_params=pltpu.CompilerParams(
            collective_id=0, has_side_effects=True, vmem_limit_bytes=52 * 1024 * 1024
        ),
        cost_estimate=pl.CostEstimate(
            flops=flops, bytes_accessed=8 * cells * snaps, transcendentals=0
        ),
        name="sketch",
    )(test_seeds, block_offsets, snapshots)


def residual_kernel(a_ref, yh_ref, yl_ref, wh_ref, wl_ref, factor_in, out_ref, factor_out):
    out_ref[...] = a_ref[...] - (
        nn(yh_ref[...], wh_ref[...]) + nn(yh_ref[...], wl_ref[...])
        + nn(yl_ref[...], wh_ref[...])
    )
    factor_out[...] = factor_in[...]


def subtract(snapshots, y_hi, y_lo, w_hi, w_lo, factor):
    cells, snaps = snapshots.shape
    tiles = 4

    def split(array):
        return pl.BlockSpec((array.shape[0] // tiles, array.shape[1]), lambda i: (i, 0))

    def whole(array):
        return pl.BlockSpec(array.shape, lambda i: (0, 0))

    return pl.pallas_call(
        residual_kernel,
        grid=(tiles,),
        out_shape=(
            jax.ShapeDtypeStruct((cells, snaps), jnp.float32),
            jax.ShapeDtypeStruct(factor.shape, jnp.float32),
        ),
        in_specs=[
            split(snapshots), split(y_hi), split(y_lo), whole(w_hi), whole(w_lo), split(factor)
        ],
        out_specs=(split(snapshots), split(factor)),
        compiler_params=pltpu.CompilerParams(vmem_limit_bytes=24 * 1024 * 1024),
        cost_estimate=pl.CostEstimate(
            flops=6 * cells * snaps * RANGE, bytes_accessed=16 * cells * snaps,
            transcendentals=0,
        ),
        name="subtract",
    )(snapshots, y_hi, y_lo, w_hi, w_lo, factor)


def local(snapshots, test_seeds, block_offsets):
    y_hi, y_lo, factor, w_hi, w_lo = sketch(snapshots, test_seeds, block_offsets)
    return subtract(snapshots, y_hi, y_lo, w_hi, w_lo, factor)


def solution(mesh):
    return jax.shard_map(
        local,
        mesh=mesh,
        in_specs=(P("space", "tm"), P(), P()),
        out_specs=(P("space", "tm"), P()),
        check_vma=False,
    )
```

```python
import functools
import math
import types

import jax
import jax.numpy as jnp
from jax import lax
from jax.experimental import pallas as pl
from jax.experimental.pallas import tpu as pltpu
from jax.sharding import PartitionSpec as P

RANGE = 512
CORANGE = 1024
BLOCK = 64
TILE = 128
GROUP = 8
STRIP = 16
CHUNKS = 16
LAG = 3

MESH = pl.DeviceIdType.MESH
PRECISE = lax.Precision.HIGHEST
SPLIT = lax.Precision.HIGH


def scramble(values):
    values = jnp.bitwise_xor(values, lax.shift_right_logical(values, jnp.int32(16)))
    values = values * 73244475
    values = jnp.bitwise_xor(values, lax.shift_right_logical(values, jnp.int32(16)))
    values = values * 73244475
    values = jnp.bitwise_xor(values, lax.shift_right_logical(values, jnp.int32(16)))
    return values


def table_strip(row_hash, col_ids, scale):
    cell_hash = scramble(jnp.bitwise_xor(row_hash, col_ids * 374761393))
    total = None
    for stream in range(4):
        hashed = scramble(cell_hash + stream * 625341585) if stream else scramble(cell_hash)
        term = jnp.bitwise_and(hashed, 16777215)
        total = term if total is None else total + term
    return (total - 33554432).astype(jnp.float32) * jnp.float32(scale)


def halves(values):
    high = values.astype(jnp.bfloat16)
    low = (values - high.astype(jnp.float32)).astype(jnp.bfloat16)
    return high, low


def nt(left_side, right_side, precision=None):
    return lax.dot_general(
        left_side, right_side, (((1,), (1,)), ((), ())), precision=precision,
        preferred_element_type=jnp.float32,
    )


def nn(left_side, right_side):
    return jnp.dot(left_side, right_side, preferred_element_type=jnp.float32)


def gram_dot(left_side, right_side):
    return lax.dot_general(
        left_side, right_side, (((0,), (0,)), ((), ())), precision=PRECISE,
        preferred_element_type=jnp.float32,
    )


def dot(left_side, right_side):
    return jnp.dot(
        left_side, right_side, precision=PRECISE, preferred_element_type=jnp.float32
    )


def identity(size):
    rows = lax.broadcasted_iota(jnp.int32, (size, size), 0)
    cols = lax.broadcasted_iota(jnp.int32, (size, size), 1)
    return jnp.where(rows == cols, 1.0, 0.0).astype(jnp.float32)

def eliminate(blocks):
    size = blocks[0].shape[0]
    eye = identity(size)
    active = [jnp.concatenate([block, eye], axis=1) for block in blocks]
    width = 2 * size
    done = [[] for _ in blocks]
    for start in range(0, size, GROUP):
        rows = size - start
        row_id = lax.broadcasted_iota(jnp.int32, (rows, width), 0)
        columns = [
            [jnp.broadcast_to(work[:, start + j : start + j + 1], (rows, width)) for j in range(GROUP)]
            for work in active
        ]
        for j in range(GROUP):
            for place, column in enumerate(columns):
                work = active[place]
                below = jnp.where(row_id > j, column[j], 0.0)
                share = below * (1.0 / column[j][j : j + 1, :])
                for i in range(j + 1, GROUP):
                    column[i] = column[i] - share * column[i][j : j + 1, :]
                active[place] = work - share * work[j : j + 1, :]
        for place, work in enumerate(active):
            top = work[:GROUP]
            r = lax.broadcasted_iota(jnp.int32, (GROUP, width), 0) + start
            c = lax.broadcasted_iota(jnp.int32, (GROUP, width), 1)
            diagonal = jnp.sum(jnp.where(r == c, top, 0.0), axis=1, keepdims=True)
            done[place].append(top / jnp.sqrt(diagonal))
            active[place] = work[GROUP:]
    return [jnp.concatenate(rows, axis=0)[:, size:] for rows in done]

def panels(tiles):
    size = tiles[0].shape[0]
    works = [jnp.concatenate([tile, identity(size)], axis=1) for tile in tiles]
    done = [[] for _ in tiles]
    for lo in range(0, size, BLOCK):
        smalls = eliminate([work[:BLOCK, lo : lo + BLOCK] for work in works])
        for place, small in enumerate(smalls):
            rows = dot(small, works[place][:BLOCK])
            done[place].append(rows[:, size:])
            if lo + BLOCK < size:
                works[place] = works[place][BLOCK:] - gram_dot(rows[:, lo + BLOCK : size], rows)
    return [jnp.concatenate(rows, axis=0) for rows in done]


def factor_tile(base, g, s, inverse, factor):
    n = g.shape[0]
    end = base + TILE
    here = slice(base, end)
    g_inv, s_inv = panels([g[here, here], s[here, here]])
    g_panel = dot(g_inv, g[here, base:])
    rows = lax.broadcasted_iota(jnp.int32, (TILE, TILE), 0)
    cols = lax.broadcasted_iota(jnp.int32, (TILE, TILE), 1)
    factor[here, here] = jnp.where(cols >= rows, g_panel[:, :TILE], 0.0)
    inverse[here, here] = s_inv
    if base:
        factor[here, :base] = jnp.zeros((TILE, base), jnp.float32)
        before = dot(s_inv, inverse[here, :base])
        inverse[here, :base] = before
    if end < n:
        factor[here, end:] = g_panel[:, TILE:]
        s_panel = dot(s_inv, s[here, end:])
        g[end:, end:] -= gram_dot(g_panel[:, TILE:], g_panel[:, TILE:])
        s[end:, end:] -= gram_dot(s_panel, s_panel)
        if base:
            inverse[end:, :base] -= gram_dot(s_panel, before)
        inverse[end:, here] = -gram_dot(s_panel, s_inv)


class Shared:
    def __init__(self, place, block, slots, target, first, sems, core_sems):
        self.__dict__.update(vars(place))
        self.block, self.slots, self.target = block, slots, target
        self.sems, self.core_sems = sems, core_sems
        self.count = block.shape[0]
        self.rows = self.count // self.squares
        half = RANGE // 2 if core_sems is not None else 0
        self.mine = self.core * half + first
        self.theirs = (1 - self.core) * half + first
        self.sends = []

    def part(self, base, index):
        return pl.ds(pl.multiple_of(base + index * self.rows, 8), self.rows)

    def copy(self, stage, hop, source, target):
        device = (lax.rem(self.space + hop, self.squares), self.tm)
        return pltpu.make_async_remote_copy(
            src_ref=source, dst_ref=target, send_sem=self.sems.at[stage, 0, hop - 1],
            recv_sem=self.sems.at[stage, 1, hop - 1], device_id=device, device_id_type=MESH,
        )

    def scatter(self):
        for hop in range(1, self.squares):
            rows = self.part(0, lax.rem(self.space + hop, self.squares))
            copy = self.copy(0, hop, self.block.at[rows], self.slots.at[hop - 1])
            copy.start()
            self.sends.append(copy)

    def reduce(self):
        for copy in list(self.sends):
            copy.wait_recv()
        total = self.block[self.part(0, self.space), :]
        for hop in range(1, self.squares):
            total = total + self.slots[hop - 1]
        own = self.part(self.mine, self.space)
        self.target[own, :] = total
        self.gathers = []
        for hop in range(1, self.squares):
            copy = self.copy(1, hop, self.target.at[own], self.target.at[own])
            copy.start()
            self.gathers.append(copy)

    def collect(self):
        for hop in range(1, self.squares):
            rows = self.part(self.mine, lax.rem(self.space + self.squares - hop, self.squares))
            self.copy(1, hop, self.target.at[rows], self.target.at[rows]).wait_recv()
        self.pass_on = []
        if self.core_sems is not None:
            copy = core_copy(self, self.target, self.mine, self.count, self.core_sems)
            copy.start()
            self.pass_on.append(copy)

    def complete(self):
        core_copy(self, self.target, self.theirs, self.count, self.core_sems).wait_recv()

    def drain(self):
        for copy in self.sends + self.gathers + self.pass_on:
            copy.wait_send()


def core_copy(place, buffer, first, count, sems):
    rows = pl.ds(pl.multiple_of(first, 8), count)
    return pltpu.make_async_remote_copy(
        src_ref=buffer.at[rows], dst_ref=buffer.at[rows], send_sem=sems.at[0],
        recv_sem=sems.at[1], device_id=place.partner, device_id_type=MESH,
    )


def sketch_kernel(
    squares, line, seeds_in, offsets_in, a_in, yh_out, yl_out, factor_out, wh_out, wl_out,
    seeds_ref, offsets_ref, a_ref, a_hi, a_lo, o_hi, o_lo, p_hi, p_lo, give, got, own_range, yc, from_left, from_right, to_left,
    yt, mt, gt, m_block, m_slots, g_slots, w_hi, w_lo, normal, rhs,
    rhs_slots, rhs_sum, inverse, factor, weights, y_hi, y_lo, wt_hi, wt_lo,
    give_sems, line_sems, ycore_sems, m_sems, mcore_sems, g_sems, gz_sems, gcore_sems, r_sems, out_sems,
):
    space = lax.axis_index("space")
    tm = lax.axis_index("tm")
    core = lax.rem(tm, 2)
    z = lax.div(tm, 2)
    cells, snaps = a_ref.shape
    half_rows = RANGE // 2
    chunk = half_rows // CHUNKS
    groups, group_rows, _ = m_block.shape
    per_group = group_rows // chunk
    partner = (space, z * 2 + 1 - core)
    right = (space, lax.rem(z + 1, line) * 2 + core)
    left = (space, lax.rem(z + line - 1, line) * 2 + core)
    peers = [(lax.rem(space + index, squares), tm) for index in range(1, squares)]
    peers += [(space, lax.rem(z + index, line) * 2 + core) for index in range(1, line)]
    peers.append(partner)
    place = types.SimpleNamespace(
        space=space, tm=tm, core=core, squares=squares, partner=partner
    )

    a_load = pltpu.make_async_copy(a_in, a_ref, out_sems.at[5])
    scalars = [
        pltpu.make_async_copy(seeds_in, seeds_ref, out_sems.at[6]),
        pltpu.make_async_copy(offsets_in, offsets_ref, out_sems.at[7]),
    ]
    for copy in scalars:
        copy.start()
    a_load.start()
    barrier = pltpu.get_barrier_semaphore()
    for device in peers:
        pl.semaphore_signal(barrier, inc=1, device_id=device, device_id_type=MESH)

    for copy in scalars:
        copy.wait()

    snap_ids = (
        offsets_ref[1] * (snaps * line * 2) + tm * snaps
        + lax.broadcasted_iota(jnp.int32, (1, snaps), 1)
    )
    snap_hash = scramble(snap_ids * 668265261 + seeds_ref[0])
    cell_ids = (
        offsets_ref[0] * (cells * squares) + space * cells
        + lax.broadcasted_iota(jnp.int32, (1, cells), 1)
    )
    cell_hash = scramble(cell_ids * 668265261 + seeds_ref[1])
    omega_scale = math.sqrt(3.0) / 16777216.0 / math.sqrt(cells * squares * snaps * line * 2)
    psi_scale = math.sqrt(3.0) / 16777216.0 / math.sqrt(cells * squares)

    def split_snapshots():
        a_load.wait()

        @pl.loop(0, cells // 128)
        def _(index):
            rows = pl.ds(pl.multiple_of(index * 128, 128), 128)
            a_hi[rows, :], a_lo[rows, :] = halves(a_ref[rows, :])

    half_range = half_rows // 2

    def omega(owner, turn):
        offset = turn * half_range

        @pl.loop(0, half_range // STRIP)
        def _(index):
            base = pl.multiple_of(index * STRIP, STRIP)
            ids = lax.broadcasted_iota(jnp.int32, (STRIP, snaps), 0) + (
                owner * half_rows + offset + base
            )
            strip = table_strip(snap_hash, ids, omega_scale)
            o_hi[pl.ds(base, STRIP), :], o_lo[pl.ds(base, STRIP), :] = halves(strip)

    def range_part(target, turn):
        offset = turn * half_range

        @pl.loop(0, cells // 512)
        def _(index):
            here = pl.ds(pl.multiple_of(index * 512, 512), 512)
            target[offset : offset + half_range, here] = (
                nt(o_hi[...], a_hi[here, :]) + nt(o_hi[...], a_lo[here, :])
                + nt(o_lo[...], a_hi[here, :])
            )

    def psi(lo, hi):
        @pl.loop(lo // STRIP, hi // STRIP)
        def _(index):
            base = pl.multiple_of(index * STRIP, STRIP)
            ids = lax.broadcasted_iota(jnp.int32, (STRIP, cells), 0) + base
            strip = table_strip(cell_hash, ids, psi_scale)
            p_hi[pl.ds(base, STRIP), :], p_lo[pl.ds(base, STRIP), :] = halves(strip)

    def line_copy(way, index, source):
        target = from_left if way == 0 else from_right
        return pltpu.make_async_remote_copy(
            src_ref=source, dst_ref=target.at[index], send_sem=line_sems.at[way, 0, index],
            recv_sem=line_sems.at[way, 1, index],
            device_id=right if way == 0 else left, device_id_type=MESH,
        )

    gives = []
    per_turn = CHUNKS // 2
    for turn in range(2):
        omega(1 - core, turn)
        if turn == 0:
            split_snapshots()
        range_part(give, turn)
        if turn == 0:
            pl.semaphore_wait(barrier, len(peers))
        rows = pl.ds(turn * half_range, half_range)
        copy = pltpu.make_async_remote_copy(
            src_ref=give.at[rows], dst_ref=got.at[rows], send_sem=give_sems.at[0, turn],
            recv_sem=give_sems.at[1, turn], device_id=partner, device_id_type=MESH,
        )
        copy.start()
        gives.append(copy)
        omega(core, turn)
        range_part(own_range, turn)
        copy.wait_recv()
        for index in range(turn * per_turn, (turn + 1) * per_turn):
            rows = pl.ds(index * chunk, chunk)
            yc[index] = own_range[rows, :] + got[rows, :]

            @pl.when(z == 0)
            def _():
                line_copy(0, index, yc.at[index]).start()

            @pl.when(z == line - 1)
            def _():
                line_copy(1, index, yc.at[index]).start()

    def line_step(step):
        index = step - 1 - LAG * (z - 1)

        @pl.when((z > 0) & (index >= 0) & (index < CHUNKS))
        def _():
            line_copy(0, index, yc.at[index]).wait_recv()
            from_left[index] = from_left[index] + yc[index]

            @pl.when(z < line - 1)
            def _():
                line_copy(0, index, from_left.at[index]).start()

        other = step - 1 - LAG * (line - 2 - z)

        @pl.when((z < line - 1) & (other >= 0) & (other < CHUNKS))
        def _():
            line_copy(1, other, yc.at[other]).wait_recv()

            @pl.when(z > 0)
            def _():
                to_left[other] = from_right[other] + yc[other]
                line_copy(1, other, to_left.at[other]).start()

        done = step - 1 - LAG * (line - 2)
        if 0 <= done < CHUNKS:
            rows = pl.ds(pl.multiple_of(core * half_rows + done * chunk, 8), chunk)

            @pl.when(z == 0)
            def _():
                yt[rows, :] = yc[done] + from_right[done]

            @pl.when(z == line - 1)
            def _():
                yt[rows, :] = from_left[done]

            @pl.when((z > 0) & (z < line - 1))
            def _():
                yt[rows, :] = from_left[done] + from_right[done]

    def line_drain():
        @pl.when(z < line - 1)
        def _():
            for index in range(CHUNKS):
                line_copy(0, index, yc.at[index]).wait_send()

        @pl.when(z > 0)
        def _():
            for index in range(CHUNKS):
                line_copy(1, index, yc.at[index]).wait_send()

    def corange(index):
        size = CORANGE // groups
        for start in range(index * size, (index + 1) * size, 256):
            here = pl.ds(start, 256)
            part = (
                nn(p_hi[here, :], a_hi[...]) + nn(p_hi[here, :], a_lo[...])
                + nn(p_lo[here, :], a_hi[...])
            )
            w_hi[here, :], w_lo[here, :] = halves(part)

    y_pass, shared = [], []

    def couple(group):
        first = group * group_rows
        copy = core_copy(place, yt, core * half_rows + first, group_rows, ycore_sems.at[group])
        copy.start()
        y_pass.append(copy)
        rows = pl.ds(pl.multiple_of(core * half_rows + first, 8), group_rows)
        high, low = halves(yt[rows, :])
        both = jnp.concatenate([high, low], axis=0)
        for tile in range(CORANGE // 256):
            here = pl.ds(tile * 256, 256)
            most = nt(both, p_hi[here, :])
            m_block[group, :, here] = (
                most[:group_rows] + most[group_rows:] + nt(high, p_lo[here, :])
            )
        total = Shared(
            place, m_block.at[group], m_slots.at[group], mt, first, m_sems.at[group],
            mcore_sems.at[group],
        )
        total.scatter()
        shared.append(total)

    steps = list(range(1, CHUNKS + 1 + LAG * (line - 2)))
    strips = CORANGE // 8
    for turn in range(8):
        psi(turn * strips, (turn + 1) * strips)
        if turn >= 1:
            line_step(steps.pop(0))
    tasks = []
    for group in range(groups):
        last = (group + 1) * per_group + LAG * (line - 2)
        while steps and steps[0] <= last:
            line_step(steps.pop(0))
            if tasks and group:
                tasks.pop(0)()
        couple(group)
        if group >= 1:
            tasks.append(shared[group - 1].reduce)
        tasks.append(functools.partial(corange, group))
        if group >= 2:
            tasks.append(shared[group - 2].collect)
    for group in range(groups):
        rows = (1 - core) * half_rows + group * group_rows
        core_copy(place, yt, rows, group_rows, ycore_sems.at[group]).wait_recv()
    g_rows = g_slots.shape[1]

    def g_part(index):
        return pl.ds(pl.multiple_of(core * half_rows + index * g_rows, 8), g_rows)

    g_own = g_part(z)
    g_slots[space] = nt(yt[g_own, :], yt[...], PRECISE)

    def g_square(hop, slot):
        return pltpu.make_async_remote_copy(
            src_ref=g_slots.at[slot], dst_ref=g_slots.at[slot], send_sem=g_sems.at[0, hop - 1],
            recv_sem=g_sems.at[1, hop - 1], device_id=(lax.rem(space + hop, squares), tm),
            device_id_type=MESH,
        )

    def g_line(hop, rows):
        return pltpu.make_async_remote_copy(
            src_ref=gt.at[rows], dst_ref=gt.at[rows], send_sem=gz_sems.at[0, hop - 1],
            recv_sem=gz_sems.at[1, hop - 1],
            device_id=(space, lax.rem(z + hop, line) * 2 + core), device_id_type=MESH,
        )

    g_sent = [g_square(hop, space) for hop in range(1, squares)]
    for copy in g_sent:
        copy.start()
    while tasks:
        tasks.pop(0)()
    shared[groups - 1].reduce()
    for hop in range(1, squares):
        g_square(hop, lax.rem(space + squares - hop, squares)).wait_recv()
    total = g_slots[0]
    for index in range(1, squares):
        total = total + g_slots[index]
    gt[g_own, :] = total
    for hop in range(1, line):
        copy = g_line(hop, g_own)
        copy.start()
        g_sent.append(copy)

    @pl.loop(0, cells // 128)
    def _(index):
        here = pl.ds(pl.multiple_of(index * 128, 128), 128)
        y_hi[here, :], y_lo[here, :] = halves(jnp.transpose(yt[:, here]))

    stores = [
        pltpu.make_async_copy(y_hi, yh_out, out_sems.at[0]),
        pltpu.make_async_copy(y_lo, yl_out, out_sems.at[1]),
    ]
    for copy in stores:
        copy.start()
    if groups > 1:
        shared[groups - 2].collect()
    shared[groups - 1].collect()
    for total in shared:
        total.complete()
    for lo in range(0, RANGE, 256):
        normal[lo : lo + 256, lo:] = nt(mt[lo : lo + 256, :], mt[lo:, :], PRECISE)
    for hop in range(1, line):
        g_line(hop, g_part(lax.rem(z + line - hop, line))).wait_recv()
    copy = core_copy(place, gt, core * half_rows, half_rows, gcore_sems)
    copy.start()
    g_sent.append(copy)

    def right_side(lo):
        here = pl.ds(lo, 256)
        m_hi, m_lo = halves(mt[here, :])
        rhs[here, :] = nn(m_hi, w_hi[...]) + nn(m_hi, w_lo[...]) + nn(m_lo, w_hi[...])

    for lo in range(0, RANGE, 256):
        right_side(lo)
    r_shared = Shared(place, rhs, rhs_slots, rhs_sum, 0, r_sems, None)
    r_shared.scatter()
    core_copy(place, gt, (1 - core) * half_rows, half_rows, gcore_sems).wait_recv()
    for copy in g_sent:
        copy.wait_send()

    for base in range(0, RANGE, TILE):
        factor_tile(base, gt, normal, inverse, factor)
        if base == 0:
            r_shared.reduce()
    stores.append(pltpu.make_async_copy(factor, factor_out, out_sems.at[2]))
    stores[-1].start()
    r_shared.collect()
    for base in range(0, RANGE, TILE):
        here, end = slice(base, base + TILE), base + TILE
        solved = dot(inverse[here, :end], rhs_sum[:end, :])
        part = gram_dot(inverse[here, :end], solved)
        if base:
            weights[:base, :] += part[:base]
        weights[here, :] = part[base:]
    wt_hi[...], wt_lo[...] = halves(weights[...])
    for source, target, sem in ((wt_hi, wh_out, 3), (wt_lo, wl_out, 4)):
        stores.append(pltpu.make_async_copy(source, target, out_sems.at[sem]))
        stores[-1].start()

    for copy in gives + y_pass:
        copy.wait_send()
    for total in shared + [r_shared]:
        total.drain()
    line_drain()
    for copy in stores:
        copy.wait()


def sketch(snapshots, test_seeds, block_offsets):
    cells, snaps = snapshots.shape
    squares = lax.axis_size("space")
    line = lax.axis_size("tm") // 2
    half_rows = RANGE // 2
    chunk = half_rows // CHUNKS
    group_rows = max(half_rows // 4, 8 * squares)
    groups = half_rows // group_rows
    f32, bf16 = jnp.float32, jnp.bfloat16
    dma = pltpu.SemaphoreType.DMA
    scratch = [
        pltpu.SMEM((2,), jnp.int32), pltpu.SMEM((2,), jnp.int32),
        pltpu.VMEM((cells, snaps), f32),
        pltpu.VMEM((cells, snaps), bf16), pltpu.VMEM((cells, snaps), bf16),
        pltpu.VMEM((half_rows // 2, snaps), bf16), pltpu.VMEM((half_rows // 2, snaps), bf16),
        pltpu.VMEM((CORANGE, cells), bf16), pltpu.VMEM((CORANGE, cells), bf16),
        pltpu.VMEM((half_rows, cells), f32), pltpu.VMEM((half_rows, cells), f32),
        pltpu.VMEM((half_rows, cells), f32),
        pltpu.VMEM((CHUNKS, chunk, cells), f32), pltpu.VMEM((CHUNKS, chunk, cells), f32),
        pltpu.VMEM((CHUNKS, chunk, cells), f32), pltpu.VMEM((CHUNKS, chunk, cells), f32),
        pltpu.VMEM((RANGE, cells), f32), pltpu.VMEM((RANGE, CORANGE), f32),
        pltpu.VMEM((RANGE, RANGE), f32),
        pltpu.VMEM((groups, group_rows, CORANGE), f32),
        pltpu.VMEM((groups, squares - 1, group_rows // squares, CORANGE), f32),
        pltpu.VMEM((squares, half_rows // line, RANGE), f32),
        pltpu.VMEM((CORANGE, snaps), bf16), pltpu.VMEM((CORANGE, snaps), bf16),
        pltpu.VMEM((RANGE, RANGE), f32), pltpu.VMEM((RANGE, snaps), f32),
        pltpu.VMEM((squares - 1, RANGE // squares, snaps), f32), pltpu.VMEM((RANGE, snaps), f32),
        pltpu.VMEM((RANGE, RANGE), f32), pltpu.VMEM((RANGE, RANGE), f32),
        pltpu.VMEM((RANGE, snaps), f32),
        pltpu.VMEM((cells, RANGE), bf16), pltpu.VMEM((cells, RANGE), bf16),
        pltpu.VMEM((RANGE, snaps), bf16), pltpu.VMEM((RANGE, snaps), bf16),
        dma((2, 2)), dma((2, 2, CHUNKS)), dma((groups, 2)),
        dma((groups, 2, 2, squares - 1)), dma((groups, 2)),
        dma((2, squares - 1)), dma((2, line - 1)), dma((2,)), dma((2, 2, squares - 1)), dma((8,)),
    ]
    flops = 2 * 3 * cells * snaps * (RANGE + CORANGE) + 2 * 9 * RANGE * RANGE * CORANGE
    return pl.pallas_call(
        functools.partial(sketch_kernel, squares, line),
        out_shape=(
            jax.ShapeDtypeStruct((cells, RANGE), bf16),
            jax.ShapeDtypeStruct((cells, RANGE), bf16),
            jax.ShapeDtypeStruct((RANGE, RANGE), f32),
            jax.ShapeDtypeStruct((RANGE, snaps), bf16),
            jax.ShapeDtypeStruct((RANGE, snaps), bf16),
        ),
        in_specs=[
            pl.BlockSpec(memory_space=pl.ANY), pl.BlockSpec(memory_space=pl.ANY),
            pl.BlockSpec(memory_space=pl.ANY),
        ],
        out_specs=(pl.BlockSpec(memory_space=pl.ANY),) * 5,
        scratch_shapes=scratch,
        compiler_params=pltpu.CompilerParams(
            collective_id=0, has_side_effects=True, vmem_limit_bytes=52 * 1024 * 1024
        ),
        cost_estimate=pl.CostEstimate(
            flops=flops, bytes_accessed=8 * cells * snaps, transcendentals=0
        ),
        name="sketch",
    )(test_seeds, block_offsets, snapshots)


def residual_kernel(a_ref, yh_ref, yl_ref, wh_ref, wl_ref, factor_in, out_ref, factor_out):
    out_ref[...] = a_ref[...] - (
        nn(yh_ref[...], wh_ref[...]) + nn(yh_ref[...], wl_ref[...])
        + nn(yl_ref[...], wh_ref[...])
    )
    factor_out[...] = factor_in[...]


def subtract(snapshots, y_hi, y_lo, w_hi, w_lo, factor):
    cells, snaps = snapshots.shape
    tiles = 4

    def split(array):
        return pl.BlockSpec((array.shape[0] // tiles, array.shape[1]), lambda i: (i, 0))

    def whole(array):
        return pl.BlockSpec(array.shape, lambda i: (0, 0))

    return pl.pallas_call(
        residual_kernel,
        grid=(tiles,),
        out_shape=(
            jax.ShapeDtypeStruct((cells, snaps), jnp.float32),
            jax.ShapeDtypeStruct(factor.shape, jnp.float32),
        ),
        in_specs=[
            split(snapshots), split(y_hi), split(y_lo), whole(w_hi), whole(w_lo), split(factor)
        ],
        out_specs=(split(snapshots), split(factor)),
        compiler_params=pltpu.CompilerParams(vmem_limit_bytes=60 * 1024 * 1024),
        cost_estimate=pl.CostEstimate(
            flops=6 * cells * snaps * RANGE, bytes_accessed=16 * cells * snaps,
            transcendentals=0,
        ),
        name="subtract",
    )(snapshots, y_hi, y_lo, w_hi, w_lo, factor)


def local(snapshots, test_seeds, block_offsets):
    y_hi, y_lo, factor, w_hi, w_lo = sketch(snapshots, test_seeds, block_offsets)
    return subtract(snapshots, y_hi, y_lo, w_hi, w_lo, factor)


def solution(mesh):
    return jax.shard_map(
        local,
        mesh=mesh,
        in_specs=(P("space", "tm"), P(), P()),
        out_specs=(P("space", "tm"), P()),
        check_vma=False,
    )
```

```python
import functools
import math
import types

import jax
import jax.numpy as jnp
from jax import lax
from jax.experimental import pallas as pl
from jax.experimental.pallas import tpu as pltpu
from jax.sharding import PartitionSpec as P

RANGE = 512
CORANGE = 1024
BLOCK = 64
TILE = 128
GROUP = 8
STRIP = 16
CHUNKS = 16
LAG = 3

MESH = pl.DeviceIdType.MESH
PRECISE = lax.Precision.HIGHEST
SPLIT = lax.Precision.HIGH


def scramble(values):
    values = jnp.bitwise_xor(values, lax.shift_right_logical(values, jnp.int32(16)))
    values = values * 73244475
    values = jnp.bitwise_xor(values, lax.shift_right_logical(values, jnp.int32(16)))
    values = values * 73244475
    values = jnp.bitwise_xor(values, lax.shift_right_logical(values, jnp.int32(16)))
    return values


def table_strip(row_hash, col_ids, scale):
    cell_hash = scramble(jnp.bitwise_xor(row_hash, col_ids * 374761393))
    total = None
    for stream in range(4):
        hashed = scramble(cell_hash + stream * 625341585) if stream else scramble(cell_hash)
        term = jnp.bitwise_and(hashed, 16777215)
        total = term if total is None else total + term
    return (total - 33554432).astype(jnp.float32) * jnp.float32(scale)


def halves(values):
    high = values.astype(jnp.bfloat16)
    low = (values - high.astype(jnp.float32)).astype(jnp.bfloat16)
    return high, low


def nt(left_side, right_side, precision=None):
    return lax.dot_general(
        left_side, right_side, (((1,), (1,)), ((), ())), precision=precision,
        preferred_element_type=jnp.float32,
    )


def nn(left_side, right_side):
    return jnp.dot(left_side, right_side, preferred_element_type=jnp.float32)


def gram_dot(left_side, right_side):
    return lax.dot_general(
        left_side, right_side, (((0,), (0,)), ((), ())), precision=PRECISE,
        preferred_element_type=jnp.float32,
    )


def dot(left_side, right_side):
    return jnp.dot(
        left_side, right_side, precision=PRECISE, preferred_element_type=jnp.float32
    )


def identity(size):
    rows = lax.broadcasted_iota(jnp.int32, (size, size), 0)
    cols = lax.broadcasted_iota(jnp.int32, (size, size), 1)
    return jnp.where(rows == cols, 1.0, 0.0).astype(jnp.float32)

def eliminate(blocks):
    size = blocks[0].shape[0]
    eye = identity(size)
    active = [jnp.concatenate([block, eye], axis=1) for block in blocks]
    width = 2 * size
    done = [[] for _ in blocks]
    for start in range(0, size, GROUP):
        rows = size - start
        row_id = lax.broadcasted_iota(jnp.int32, (rows, width), 0)
        columns = [
            [jnp.broadcast_to(work[:, start + j : start + j + 1], (rows, width)) for j in range(GROUP)]
            for work in active
        ]
        for j in range(GROUP):
            for place, column in enumerate(columns):
                work = active[place]
                below = jnp.where(row_id > j, column[j], 0.0)
                share = below * (1.0 / column[j][j : j + 1, :])
                for i in range(j + 1, GROUP):
                    column[i] = column[i] - share * column[i][j : j + 1, :]
                active[place] = work - share * work[j : j + 1, :]
        for place, work in enumerate(active):
            top = work[:GROUP]
            r = lax.broadcasted_iota(jnp.int32, (GROUP, width), 0) + start
            c = lax.broadcasted_iota(jnp.int32, (GROUP, width), 1)
            diagonal = jnp.sum(jnp.where(r == c, top, 0.0), axis=1, keepdims=True)
            done[place].append(top / jnp.sqrt(diagonal))
            active[place] = work[GROUP:]
    return [jnp.concatenate(rows, axis=0)[:, size:] for rows in done]

def panels(tiles):
    size = tiles[0].shape[0]
    works = [jnp.concatenate([tile, identity(size)], axis=1) for tile in tiles]
    done = [[] for _ in tiles]
    for lo in range(0, size, BLOCK):
        smalls = eliminate([work[:BLOCK, lo : lo + BLOCK] for work in works])
        for place, small in enumerate(smalls):
            rows = dot(small, works[place][:BLOCK])
            done[place].append(rows[:, size:])
            if lo + BLOCK < size:
                works[place] = works[place][BLOCK:] - gram_dot(rows[:, lo + BLOCK : size], rows)
    return [jnp.concatenate(rows, axis=0) for rows in done]


def factor_tile(base, g, s, inverse, factor):
    n = g.shape[0]
    end = base + TILE
    here = slice(base, end)
    g_inv, s_inv = panels([g[here, here], s[here, here]])
    g_panel = dot(g_inv, g[here, base:])
    rows = lax.broadcasted_iota(jnp.int32, (TILE, TILE), 0)
    cols = lax.broadcasted_iota(jnp.int32, (TILE, TILE), 1)
    factor[here, here] = jnp.where(cols >= rows, g_panel[:, :TILE], 0.0)
    inverse[here, here] = s_inv
    if base:
        factor[here, :base] = jnp.zeros((TILE, base), jnp.float32)
        before = dot(s_inv, inverse[here, :base])
        inverse[here, :base] = before
    if end < n:
        factor[here, end:] = g_panel[:, TILE:]
        s_panel = dot(s_inv, s[here, end:])
        g[end:, end:] -= gram_dot(g_panel[:, TILE:], g_panel[:, TILE:])
        s[end:, end:] -= gram_dot(s_panel, s_panel)
        if base:
            inverse[end:, :base] -= gram_dot(s_panel, before)
        inverse[end:, here] = -gram_dot(s_panel, s_inv)


class Shared:
    def __init__(self, place, block, slots, target, first, sems, core_sems):
        self.__dict__.update(vars(place))
        self.block, self.slots, self.target = block, slots, target
        self.sems, self.core_sems = sems, core_sems
        self.count = block.shape[0]
        self.rows = self.count // self.squares
        half = RANGE // 2 if core_sems is not None else 0
        self.mine = self.core * half + first
        self.theirs = (1 - self.core) * half + first
        self.sends = []

    def part(self, base, index):
        return pl.ds(pl.multiple_of(base + index * self.rows, 8), self.rows)

    def copy(self, stage, hop, source, target):
        device = (lax.rem(self.space + hop, self.squares), self.tm)
        return pltpu.make_async_remote_copy(
            src_ref=source, dst_ref=target, send_sem=self.sems.at[stage, 0, hop - 1],
            recv_sem=self.sems.at[stage, 1, hop - 1], device_id=device, device_id_type=MESH,
        )

    def scatter(self):
        for hop in range(1, self.squares):
            rows = self.part(0, lax.rem(self.space + hop, self.squares))
            copy = self.copy(0, hop, self.block.at[rows], self.slots.at[hop - 1])
            copy.start()
            self.sends.append(copy)

    def reduce(self):
        for copy in list(self.sends):
            copy.wait_recv()
        total = self.block[self.part(0, self.space), :]
        for hop in range(1, self.squares):
            total = total + self.slots[hop - 1]
        own = self.part(self.mine, self.space)
        self.target[own, :] = total
        self.gathers = []
        for hop in range(1, self.squares):
            copy = self.copy(1, hop, self.target.at[own], self.target.at[own])
            copy.start()
            self.gathers.append(copy)

    def collect(self):
        for hop in range(1, self.squares):
            rows = self.part(self.mine, lax.rem(self.space + self.squares - hop, self.squares))
            self.copy(1, hop, self.target.at[rows], self.target.at[rows]).wait_recv()
        self.pass_on = []
        if self.core_sems is not None:
            copy = core_copy(self, self.target, self.mine, self.count, self.core_sems)
            copy.start()
            self.pass_on.append(copy)

    def complete(self):
        core_copy(self, self.target, self.theirs, self.count, self.core_sems).wait_recv()

    def drain(self):
        for copy in self.sends + self.gathers + self.pass_on:
            copy.wait_send()


def core_copy(place, buffer, first, count, sems):
    rows = pl.ds(pl.multiple_of(first, 8), count)
    return pltpu.make_async_remote_copy(
        src_ref=buffer.at[rows], dst_ref=buffer.at[rows], send_sem=sems.at[0],
        recv_sem=sems.at[1], device_id=place.partner, device_id_type=MESH,
    )


def sketch_kernel(
    squares, line, seeds_in, offsets_in, a_in, yh_out, yl_out, factor_out, wh_out, wl_out,
    seeds_ref, offsets_ref, a_ref, a_hi, a_lo, o_hi, o_lo, p_hi, p_lo, give, got, own_range, yc, from_left, from_right, to_left,
    yt, mt, gt, m_block, m_slots, g_slots, w_hi, w_lo, normal, rhs,
    rhs_slots, rhs_sum, inverse, factor, weights, y_hi, y_lo, wt_hi, wt_lo,
    give_sems, line_sems, ycore_sems, m_sems, mcore_sems, g_sems, gz_sems, gcore_sems, r_sems, out_sems,
):
    space = lax.axis_index("space")
    tm = lax.axis_index("tm")
    core = lax.rem(tm, 2)
    z = lax.div(tm, 2)
    cells, snaps = a_ref.shape
    half_rows = RANGE // 2
    chunk = half_rows // CHUNKS
    groups, group_rows, _ = m_block.shape
    per_group = group_rows // chunk
    partner = (space, z * 2 + 1 - core)
    right = (space, lax.rem(z + 1, line) * 2 + core)
    left = (space, lax.rem(z + line - 1, line) * 2 + core)
    peers = [(lax.rem(space + index, squares), tm) for index in range(1, squares)]
    peers += [(space, lax.rem(z + index, line) * 2 + core) for index in range(1, line)]
    peers.append(partner)
    place = types.SimpleNamespace(
        space=space, tm=tm, core=core, squares=squares, partner=partner
    )

    a_load = pltpu.make_async_copy(a_in, a_ref, out_sems.at[5])
    scalars = [
        pltpu.make_async_copy(seeds_in, seeds_ref, out_sems.at[6]),
        pltpu.make_async_copy(offsets_in, offsets_ref, out_sems.at[7]),
    ]
    for copy in scalars:
        copy.start()
    a_load.start()
    barrier = pltpu.get_barrier_semaphore()
    for device in peers:
        pl.semaphore_signal(barrier, inc=1, device_id=device, device_id_type=MESH)

    for copy in scalars:
        copy.wait()

    snap_ids = (
        offsets_ref[1] * (snaps * line * 2) + tm * snaps
        + lax.broadcasted_iota(jnp.int32, (1, snaps), 1)
    )
    snap_hash = scramble(snap_ids * 668265261 + seeds_ref[0])
    cell_ids = (
        offsets_ref[0] * (cells * squares) + space * cells
        + lax.broadcasted_iota(jnp.int32, (1, cells), 1)
    )
    cell_hash = scramble(cell_ids * 668265261 + seeds_ref[1])
    omega_scale = math.sqrt(3.0) / 16777216.0 / math.sqrt(cells * squares * snaps * line * 2)
    psi_scale = math.sqrt(3.0) / 16777216.0 / math.sqrt(cells * squares)

    def split_snapshots():
        a_load.wait()

        @pl.loop(0, cells // 128)
        def _(index):
            rows = pl.ds(pl.multiple_of(index * 128, 128), 128)
            a_hi[rows, :], a_lo[rows, :] = halves(a_ref[rows, :])

    half_range = half_rows // 2

    def omega(owner, turn):
        offset = turn * half_range

        @pl.loop(0, half_range // STRIP)
        def _(index):
            base = pl.multiple_of(index * STRIP, STRIP)
            ids = lax.broadcasted_iota(jnp.int32, (STRIP, snaps), 0) + (
                owner * half_rows + offset + base
            )
            strip = table_strip(snap_hash, ids, omega_scale)
            o_hi[pl.ds(base, STRIP), :], o_lo[pl.ds(base, STRIP), :] = halves(strip)

    def range_part(target, turn):
        offset = turn * half_range

        @pl.loop(0, cells // 512)
        def _(index):
            here = pl.ds(pl.multiple_of(index * 512, 512), 512)
            target[offset : offset + half_range, here] = (
                nt(o_hi[...], a_hi[here, :]) + nt(o_hi[...], a_lo[here, :])
                + nt(o_lo[...], a_hi[here, :])
            )

    def psi(lo, hi):
        @pl.loop(lo // STRIP, hi // STRIP)
        def _(index):
            base = pl.multiple_of(index * STRIP, STRIP)
            ids = lax.broadcasted_iota(jnp.int32, (STRIP, cells), 0) + base
            strip = table_strip(cell_hash, ids, psi_scale)
            p_hi[pl.ds(base, STRIP), :], p_lo[pl.ds(base, STRIP), :] = halves(strip)

    def line_copy(way, index, source):
        target = from_left if way == 0 else from_right
        return pltpu.make_async_remote_copy(
            src_ref=source, dst_ref=target.at[index], send_sem=line_sems.at[way, 0, index],
            recv_sem=line_sems.at[way, 1, index],
            device_id=right if way == 0 else left, device_id_type=MESH,
        )

    gives = []
    per_turn = CHUNKS // 2
    for turn in range(2):
        omega(1 - core, turn)
        if turn == 0:
            split_snapshots()
        range_part(give, turn)
        if turn == 0:
            pl.semaphore_wait(barrier, len(peers))
        rows = pl.ds(turn * half_range, half_range)
        copy = pltpu.make_async_remote_copy(
            src_ref=give.at[rows], dst_ref=got.at[rows], send_sem=give_sems.at[0, turn],
            recv_sem=give_sems.at[1, turn], device_id=partner, device_id_type=MESH,
        )
        copy.start()
        gives.append(copy)
        omega(core, turn)
        range_part(own_range, turn)
        copy.wait_recv()
        for index in range(turn * per_turn, (turn + 1) * per_turn):
            rows = pl.ds(index * chunk, chunk)
            yc[index] = own_range[rows, :] + got[rows, :]

            @pl.when(z == 0)
            def _():
                line_copy(0, index, yc.at[index]).start()

            @pl.when(z == line - 1)
            def _():
                line_copy(1, index, yc.at[index]).start()

    def line_step(step):
        index = step - 1 - LAG * (z - 1)

        @pl.when((z > 0) & (index >= 0) & (index < CHUNKS))
        def _():
            line_copy(0, index, yc.at[index]).wait_recv()
            from_left[index] = from_left[index] + yc[index]

            @pl.when(z < line - 1)
            def _():
                line_copy(0, index, from_left.at[index]).start()

        other = step - 1 - LAG * (line - 2 - z)

        @pl.when((z < line - 1) & (other >= 0) & (other < CHUNKS))
        def _():
            line_copy(1, other, yc.at[other]).wait_recv()

            @pl.when(z > 0)
            def _():
                to_left[other] = from_right[other] + yc[other]
                line_copy(1, other, to_left.at[other]).start()

        done = step - 1 - LAG * (line - 2)
        if 0 <= done < CHUNKS:
            rows = pl.ds(pl.multiple_of(core * half_rows + done * chunk, 8), chunk)

            @pl.when(z == 0)
            def _():
                yt[rows, :] = yc[done] + from_right[done]

            @pl.when(z == line - 1)
            def _():
                yt[rows, :] = from_left[done]

            @pl.when((z > 0) & (z < line - 1))
            def _():
                yt[rows, :] = from_left[done] + from_right[done]

    def line_drain():
        @pl.when(z < line - 1)
        def _():
            for index in range(CHUNKS):
                line_copy(0, index, yc.at[index]).wait_send()

        @pl.when(z > 0)
        def _():
            for index in range(CHUNKS):
                line_copy(1, index, yc.at[index]).wait_send()

    def corange(index):
        size = CORANGE // groups
        for start in range(index * size, (index + 1) * size, 256):
            here = pl.ds(start, 256)
            part = (
                nn(p_hi[here, :], a_hi[...]) + nn(p_hi[here, :], a_lo[...])
                + nn(p_lo[here, :], a_hi[...])
            )
            w_hi[here, :], w_lo[here, :] = halves(part)

    y_pass, shared = [], []

    def couple(group):
        first = group * group_rows
        copy = core_copy(place, yt, core * half_rows + first, group_rows, ycore_sems.at[group])
        copy.start()
        y_pass.append(copy)
        rows = pl.ds(pl.multiple_of(core * half_rows + first, 8), group_rows)
        high, low = halves(yt[rows, :])
        both = jnp.concatenate([high, low], axis=0)
        for tile in range(CORANGE // 256):
            here = pl.ds(tile * 256, 256)
            most = nt(both, p_hi[here, :])
            m_block[group, :, here] = (
                most[:group_rows] + most[group_rows:] + nt(high, p_lo[here, :])
            )
        total = Shared(
            place, m_block.at[group], m_slots.at[group], mt, first, m_sems.at[group],
            mcore_sems.at[group],
        )
        total.scatter()
        shared.append(total)

    steps = list(range(1, CHUNKS + 1 + LAG * (line - 2)))
    strips = CORANGE // 8
    for turn in range(8):
        psi(turn * strips, (turn + 1) * strips)
        if turn >= 1:
            line_step(steps.pop(0))
    tasks = []
    for group in range(groups):
        last = (group + 1) * per_group + LAG * (line - 2)
        while steps and steps[0] <= last:
            line_step(steps.pop(0))
            if tasks and group:
                tasks.pop(0)()
        couple(group)
        if group >= 1:
            tasks.append(shared[group - 1].reduce)
        tasks.append(functools.partial(corange, group))
        if group >= 2:
            tasks.append(shared[group - 2].collect)
    for group in range(groups):
        rows = (1 - core) * half_rows + group * group_rows
        core_copy(place, yt, rows, group_rows, ycore_sems.at[group]).wait_recv()
    g_rows = g_slots.shape[1]

    def g_part(index):
        return pl.ds(pl.multiple_of(core * half_rows + index * g_rows, 8), g_rows)

    g_own = g_part(z)
    g_slots[space] = nt(yt[g_own, :], yt[...], PRECISE)

    def g_square(hop, slot):
        return pltpu.make_async_remote_copy(
            src_ref=g_slots.at[slot], dst_ref=g_slots.at[slot], send_sem=g_sems.at[0, hop - 1],
            recv_sem=g_sems.at[1, hop - 1], device_id=(lax.rem(space + hop, squares), tm),
            device_id_type=MESH,
        )

    def g_line(hop, rows):
        return pltpu.make_async_remote_copy(
            src_ref=gt.at[rows], dst_ref=gt.at[rows], send_sem=gz_sems.at[0, hop - 1],
            recv_sem=gz_sems.at[1, hop - 1],
            device_id=(space, lax.rem(z + hop, line) * 2 + core), device_id_type=MESH,
        )

    g_sent = [g_square(hop, space) for hop in range(1, squares)]
    for copy in g_sent:
        copy.start()
    while tasks:
        tasks.pop(0)()
    shared[groups - 1].reduce()
    for hop in range(1, squares):
        g_square(hop, lax.rem(space + squares - hop, squares)).wait_recv()
    total = g_slots[0]
    for index in range(1, squares):
        total = total + g_slots[index]
    gt[g_own, :] = total
    for hop in range(1, line):
        copy = g_line(hop, g_own)
        copy.start()
        g_sent.append(copy)

    @pl.loop(0, cells // 128)
    def _(index):
        here = pl.ds(pl.multiple_of(index * 128, 128), 128)
        y_hi[here, :], y_lo[here, :] = halves(jnp.transpose(yt[:, here]))

    stores = [
        pltpu.make_async_copy(y_hi, yh_out, out_sems.at[0]),
        pltpu.make_async_copy(y_lo, yl_out, out_sems.at[1]),
    ]
    for copy in stores:
        copy.start()
    if groups > 1:
        shared[groups - 2].collect()
    shared[groups - 1].collect()
    for total in shared:
        total.complete()
    for lo in range(0, RANGE, 256):
        normal[lo : lo + 256, lo:] = nt(mt[lo : lo + 256, :], mt[lo:, :], PRECISE)
    def right_side(lo):
        here = pl.ds(lo, 256)
        m_hi, m_lo = halves(mt[here, :])
        rhs[here, :] = nn(m_hi, w_hi[...]) + nn(m_hi, w_lo[...]) + nn(m_lo, w_hi[...])

    for lo in range(0, RANGE, 256):
        right_side(lo)
    r_shared = Shared(place, rhs, rhs_slots, rhs_sum, 0, r_sems, None)
    r_shared.scatter()
    for hop in range(1, line):
        g_line(hop, g_part(lax.rem(z + line - hop, line))).wait_recv()
    copy = core_copy(place, gt, core * half_rows, half_rows, gcore_sems)
    copy.start()
    g_sent.append(copy)
    core_copy(place, gt, (1 - core) * half_rows, half_rows, gcore_sems).wait_recv()
    for copy in g_sent:
        copy.wait_send()

    for base in range(0, RANGE, TILE):
        factor_tile(base, gt, normal, inverse, factor)
        if base == TILE:
            r_shared.reduce()
    stores.append(pltpu.make_async_copy(factor, factor_out, out_sems.at[2]))
    stores[-1].start()
    r_shared.collect()
    for base in range(0, RANGE, TILE):
        here, end = slice(base, base + TILE), base + TILE
        solved = dot(inverse[here, :end], rhs_sum[:end, :])
        part = gram_dot(inverse[here, :end], solved)
        if base:
            weights[:base, :] += part[:base]
        weights[here, :] = part[base:]
    wt_hi[...], wt_lo[...] = halves(weights[...])
    for source, target, sem in ((wt_hi, wh_out, 3), (wt_lo, wl_out, 4)):
        stores.append(pltpu.make_async_copy(source, target, out_sems.at[sem]))
        stores[-1].start()

    for copy in gives + y_pass:
        copy.wait_send()
    for total in shared + [r_shared]:
        total.drain()
    line_drain()
    for copy in stores:
        copy.wait()


def sketch(snapshots, test_seeds, block_offsets):
    cells, snaps = snapshots.shape
    squares = lax.axis_size("space")
    line = lax.axis_size("tm") // 2
    half_rows = RANGE // 2
    chunk = half_rows // CHUNKS
    group_rows = max(half_rows // 4, 8 * squares)
    groups = half_rows // group_rows
    f32, bf16 = jnp.float32, jnp.bfloat16
    dma = pltpu.SemaphoreType.DMA
    scratch = [
        pltpu.SMEM((2,), jnp.int32), pltpu.SMEM((2,), jnp.int32),
        pltpu.VMEM((cells, snaps), f32),
        pltpu.VMEM((cells, snaps), bf16), pltpu.VMEM((cells, snaps), bf16),
        pltpu.VMEM((half_rows // 2, snaps), bf16), pltpu.VMEM((half_rows // 2, snaps), bf16),
        pltpu.VMEM((CORANGE, cells), bf16), pltpu.VMEM((CORANGE, cells), bf16),
        pltpu.VMEM((half_rows, cells), f32), pltpu.VMEM((half_rows, cells), f32),
        pltpu.VMEM((half_rows, cells), f32),
        pltpu.VMEM((CHUNKS, chunk, cells), f32), pltpu.VMEM((CHUNKS, chunk, cells), f32),
        pltpu.VMEM((CHUNKS, chunk, cells), f32), pltpu.VMEM((CHUNKS, chunk, cells), f32),
        pltpu.VMEM((RANGE, cells), f32), pltpu.VMEM((RANGE, CORANGE), f32),
        pltpu.VMEM((RANGE, RANGE), f32),
        pltpu.VMEM((groups, group_rows, CORANGE), f32),
        pltpu.VMEM((groups, squares - 1, group_rows // squares, CORANGE), f32),
        pltpu.VMEM((squares, half_rows // line, RANGE), f32),
        pltpu.VMEM((CORANGE, snaps), bf16), pltpu.VMEM((CORANGE, snaps), bf16),
        pltpu.VMEM((RANGE, RANGE), f32), pltpu.VMEM((RANGE, snaps), f32),
        pltpu.VMEM((squares - 1, RANGE // squares, snaps), f32), pltpu.VMEM((RANGE, snaps), f32),
        pltpu.VMEM((RANGE, RANGE), f32), pltpu.VMEM((RANGE, RANGE), f32),
        pltpu.VMEM((RANGE, snaps), f32),
        pltpu.VMEM((cells, RANGE), bf16), pltpu.VMEM((cells, RANGE), bf16),
        pltpu.VMEM((RANGE, snaps), bf16), pltpu.VMEM((RANGE, snaps), bf16),
        dma((2, 2)), dma((2, 2, CHUNKS)), dma((groups, 2)),
        dma((groups, 2, 2, squares - 1)), dma((groups, 2)),
        dma((2, squares - 1)), dma((2, line - 1)), dma((2,)), dma((2, 2, squares - 1)), dma((8,)),
    ]
    flops = 2 * 3 * cells * snaps * (RANGE + CORANGE) + 2 * 9 * RANGE * RANGE * CORANGE
    return pl.pallas_call(
        functools.partial(sketch_kernel, squares, line),
        out_shape=(
            jax.ShapeDtypeStruct((cells, RANGE), bf16),
            jax.ShapeDtypeStruct((cells, RANGE), bf16),
            jax.ShapeDtypeStruct((RANGE, RANGE), f32),
            jax.ShapeDtypeStruct((RANGE, snaps), bf16),
            jax.ShapeDtypeStruct((RANGE, snaps), bf16),
        ),
        in_specs=[
            pl.BlockSpec(memory_space=pl.ANY), pl.BlockSpec(memory_space=pl.ANY),
            pl.BlockSpec(memory_space=pl.ANY),
        ],
        out_specs=(pl.BlockSpec(memory_space=pl.ANY),) * 5,
        scratch_shapes=scratch,
        compiler_params=pltpu.CompilerParams(
            collective_id=0, has_side_effects=True, vmem_limit_bytes=40 * 1024 * 1024
        ),
        cost_estimate=pl.CostEstimate(
            flops=flops, bytes_accessed=8 * cells * snaps, transcendentals=0
        ),
        name="sketch",
    )(test_seeds, block_offsets, snapshots)


def residual_kernel(a_ref, yh_ref, yl_ref, wh_ref, wl_ref, factor_in, out_ref, factor_out):
    out_ref[...] = a_ref[...] - (
        nn(yh_ref[...], wh_ref[...]) + nn(yh_ref[...], wl_ref[...])
        + nn(yl_ref[...], wh_ref[...])
    )
    factor_out[...] = factor_in[...]


def subtract(snapshots, y_hi, y_lo, w_hi, w_lo, factor):
    cells, snaps = snapshots.shape
    tiles = 4

    def split(array):
        return pl.BlockSpec((array.shape[0] // tiles, array.shape[1]), lambda i: (i, 0))

    def whole(array):
        return pl.BlockSpec(array.shape, lambda i: (0, 0))

    return pl.pallas_call(
        residual_kernel,
        grid=(tiles,),
        out_shape=(
            jax.ShapeDtypeStruct((cells, snaps), jnp.float32),
            jax.ShapeDtypeStruct(factor.shape, jnp.float32),
        ),
        in_specs=[
            split(snapshots), split(y_hi), split(y_lo), whole(w_hi), whole(w_lo), split(factor)
        ],
        out_specs=(split(snapshots), split(factor)),
        compiler_params=pltpu.CompilerParams(vmem_limit_bytes=16 * 1024 * 1024),
        cost_estimate=pl.CostEstimate(
            flops=6 * cells * snaps * RANGE, bytes_accessed=16 * cells * snaps,
            transcendentals=0,
        ),
        name="subtract",
    )(snapshots, y_hi, y_lo, w_hi, w_lo, factor)


def local(snapshots, test_seeds, block_offsets):
    y_hi, y_lo, factor, w_hi, w_lo = sketch(snapshots, test_seeds, block_offsets)
    return subtract(snapshots, y_hi, y_lo, w_hi, w_lo, factor)


def solution(mesh):
    return jax.shard_map(
        local,
        mesh=mesh,
        in_specs=(P("space", "tm"), P(), P()),
        out_specs=(P("space", "tm"), P()),
        check_vma=False,
    )
```

```python
import functools
import math
import types

import jax
import jax.numpy as jnp
from jax import lax
from jax.experimental import pallas as pl
from jax.experimental.pallas import tpu as pltpu
from jax.sharding import PartitionSpec as P

RANGE = 512
CORANGE = 1024
BLOCK = 64
TILE = 128
GROUP = 8
STRIP = 16
CHUNKS = 16
LAG = 3

MESH = pl.DeviceIdType.MESH
PRECISE = lax.Precision.HIGHEST
SPLIT = lax.Precision.HIGH


def scramble(values):
    values = jnp.bitwise_xor(values, lax.shift_right_logical(values, jnp.int32(16)))
    values = values * 73244475
    values = jnp.bitwise_xor(values, lax.shift_right_logical(values, jnp.int32(16)))
    values = values * 73244475
    values = jnp.bitwise_xor(values, lax.shift_right_logical(values, jnp.int32(16)))
    return values


def table_strip(row_hash, col_ids, scale):
    cell_hash = scramble(jnp.bitwise_xor(row_hash, col_ids * 374761393))
    total = None
    for stream in range(4):
        hashed = scramble(cell_hash + stream * 625341585) if stream else scramble(cell_hash)
        term = jnp.bitwise_and(hashed, 16777215)
        total = term if total is None else total + term
    return (total - 33554432).astype(jnp.float32) * jnp.float32(scale)


def halves(values):
    high = values.astype(jnp.bfloat16)
    low = (values - high.astype(jnp.float32)).astype(jnp.bfloat16)
    return high, low


def nt(left_side, right_side, precision=None):
    return lax.dot_general(
        left_side, right_side, (((1,), (1,)), ((), ())), precision=precision,
        preferred_element_type=jnp.float32,
    )


def nn(left_side, right_side):
    return jnp.dot(left_side, right_side, preferred_element_type=jnp.float32)


def gram_dot(left_side, right_side):
    return lax.dot_general(
        left_side, right_side, (((0,), (0,)), ((), ())), precision=PRECISE,
        preferred_element_type=jnp.float32,
    )


def dot(left_side, right_side):
    return jnp.dot(
        left_side, right_side, precision=PRECISE, preferred_element_type=jnp.float32
    )


def identity(size):
    rows = lax.broadcasted_iota(jnp.int32, (size, size), 0)
    cols = lax.broadcasted_iota(jnp.int32, (size, size), 1)
    return jnp.where(rows == cols, 1.0, 0.0).astype(jnp.float32)

def eliminate(blocks):
    size = blocks[0].shape[0]
    eye = identity(size)
    active = [jnp.concatenate([block, eye], axis=1) for block in blocks]
    width = 2 * size
    done = [[] for _ in blocks]
    for start in range(0, size, GROUP):
        rows = size - start
        row_id = lax.broadcasted_iota(jnp.int32, (rows, width), 0)
        columns = [
            [jnp.broadcast_to(work[:, start + j : start + j + 1], (rows, width)) for j in range(GROUP)]
            for work in active
        ]
        for j in range(GROUP):
            for place, column in enumerate(columns):
                work = active[place]
                below = jnp.where(row_id > j, column[j], 0.0)
                share = below * (1.0 / column[j][j : j + 1, :])
                for i in range(j + 1, GROUP):
                    column[i] = column[i] - share * column[i][j : j + 1, :]
                active[place] = work - share * work[j : j + 1, :]
        for place, work in enumerate(active):
            top = work[:GROUP]
            r = lax.broadcasted_iota(jnp.int32, (GROUP, width), 0) + start
            c = lax.broadcasted_iota(jnp.int32, (GROUP, width), 1)
            diagonal = jnp.sum(jnp.where(r == c, top, 0.0), axis=1, keepdims=True)
            done[place].append(top / jnp.sqrt(diagonal))
            active[place] = work[GROUP:]
    return [jnp.concatenate(rows, axis=0)[:, size:] for rows in done]

def panels(tiles):
    size = tiles[0].shape[0]
    works = [jnp.concatenate([tile, identity(size)], axis=1) for tile in tiles]
    done = [[] for _ in tiles]
    for lo in range(0, size, BLOCK):
        smalls = eliminate([work[:BLOCK, lo : lo + BLOCK] for work in works])
        for place, small in enumerate(smalls):
            rows = dot(small, works[place][:BLOCK])
            done[place].append(rows[:, size:])
            if lo + BLOCK < size:
                works[place] = works[place][BLOCK:] - gram_dot(rows[:, lo + BLOCK : size], rows)
    return [jnp.concatenate(rows, axis=0) for rows in done]


def factor_tile(base, tiles, g, s, inverse, factor):
    n = g.shape[0]
    end = base + TILE
    here, following = slice(base, end), slice(end, end + TILE)
    g_inv, s_inv = panels(tiles)
    if end < n:
        g_first, s_first = dot(g_inv, g[here, following]), dot(s_inv, s[here, following])
        tiles = [
            g[following, following] - gram_dot(g_first, g_first),
            s[following, following] - gram_dot(s_first, s_first),
        ]
    rows = lax.broadcasted_iota(jnp.int32, (TILE, TILE), 0)
    cols = lax.broadcasted_iota(jnp.int32, (TILE, TILE), 1)
    factor[here, here] = jnp.where(cols >= rows, dot(g_inv, g[here, here]), 0.0)
    inverse[here, here] = s_inv
    if base:
        factor[here, :base] = jnp.zeros((TILE, base), jnp.float32)
        before = dot(s_inv, inverse[here, :base])
        inverse[here, :base] = before
    if end < n:
        factor[here, following] = g_first
        s_panel, rest = s_first, end + TILE
        if rest < n:
            g_rest, s_rest = dot(g_inv, g[here, rest:]), dot(s_inv, s[here, rest:])
            factor[here, rest:] = g_rest
            s_panel = jnp.concatenate([s_first, s_rest], axis=1)
            g[following, rest:] -= gram_dot(g_first, g_rest)
            s[following, rest:] -= gram_dot(s_first, s_rest)
            g[rest:, rest:] -= gram_dot(g_rest, g_rest)
            s[rest:, rest:] -= gram_dot(s_rest, s_rest)
        g[following, following] = tiles[0]
        if base:
            inverse[end:, :base] -= gram_dot(s_panel, before)
        inverse[end:, here] = -gram_dot(s_panel, s_inv)
    return tiles


class Shared:
    def __init__(self, place, block, slots, target, first, sems, core_sems):
        self.__dict__.update(vars(place))
        self.block, self.slots, self.target = block, slots, target
        self.sems, self.core_sems = sems, core_sems
        self.count = block.shape[0]
        self.rows = self.count // self.squares
        half = RANGE // 2 if core_sems is not None else 0
        self.mine = self.core * half + first
        self.theirs = (1 - self.core) * half + first
        self.sends = []

    def part(self, base, index):
        return pl.ds(pl.multiple_of(base + index * self.rows, 8), self.rows)

    def copy(self, stage, hop, source, target):
        device = (lax.rem(self.space + hop, self.squares), self.tm)
        return pltpu.make_async_remote_copy(
            src_ref=source, dst_ref=target, send_sem=self.sems.at[stage, 0, hop - 1],
            recv_sem=self.sems.at[stage, 1, hop - 1], device_id=device, device_id_type=MESH,
        )

    def scatter(self):
        for hop in range(1, self.squares):
            rows = self.part(0, lax.rem(self.space + hop, self.squares))
            copy = self.copy(0, hop, self.block.at[rows], self.slots.at[hop - 1])
            copy.start()
            self.sends.append(copy)

    def reduce(self):
        for copy in list(self.sends):
            copy.wait_recv()
        total = self.block[self.part(0, self.space), :]
        for hop in range(1, self.squares):
            total = total + self.slots[hop - 1]
        own = self.part(self.mine, self.space)
        self.target[own, :] = total
        self.gathers = []
        for hop in range(1, self.squares):
            copy = self.copy(1, hop, self.target.at[own], self.target.at[own])
            copy.start()
            self.gathers.append(copy)

    def collect(self):
        for hop in range(1, self.squares):
            rows = self.part(self.mine, lax.rem(self.space + self.squares - hop, self.squares))
            self.copy(1, hop, self.target.at[rows], self.target.at[rows]).wait_recv()
        self.pass_on = []
        if self.core_sems is not None:
            copy = core_copy(self, self.target, self.mine, self.count, self.core_sems)
            copy.start()
            self.pass_on.append(copy)

    def complete(self):
        core_copy(self, self.target, self.theirs, self.count, self.core_sems).wait_recv()

    def drain(self):
        for copy in self.sends + self.gathers + self.pass_on:
            copy.wait_send()


def core_copy(place, buffer, first, count, sems):
    rows = pl.ds(pl.multiple_of(first, 8), count)
    return pltpu.make_async_remote_copy(
        src_ref=buffer.at[rows], dst_ref=buffer.at[rows], send_sem=sems.at[0],
        recv_sem=sems.at[1], device_id=place.partner, device_id_type=MESH,
    )


def sketch_kernel(
    squares, line, seeds_in, offsets_in, a_in, yh_out, yl_out, factor_out, wh_out, wl_out,
    seeds_ref, offsets_ref, a_ref, a_hi, a_lo, o_hi, o_lo, p_hi, p_lo, give, got, own_range, yc, from_left, from_right, to_left,
    yt, mt, gt, m_block, m_slots, g_slots, w_hi, w_lo, normal, rhs,
    rhs_slots, rhs_sum, inverse, factor, weights, y_hi, y_lo, wt_hi, wt_lo,
    give_sems, line_sems, ycore_sems, m_sems, mcore_sems, g_sems, gz_sems, gcore_sems, r_sems, out_sems,
):
    space = lax.axis_index("space")
    tm = lax.axis_index("tm")
    core = lax.rem(tm, 2)
    z = lax.div(tm, 2)
    cells, snaps = a_ref.shape
    half_rows = RANGE // 2
    chunk = half_rows // CHUNKS
    groups, group_rows, _ = m_block.shape
    per_group = group_rows // chunk
    partner = (space, z * 2 + 1 - core)
    right = (space, lax.rem(z + 1, line) * 2 + core)
    left = (space, lax.rem(z + line - 1, line) * 2 + core)
    peers = [(lax.rem(space + index, squares), tm) for index in range(1, squares)]
    peers += [(space, lax.rem(z + index, line) * 2 + core) for index in range(1, line)]
    peers.append(partner)
    place = types.SimpleNamespace(
        space=space, tm=tm, core=core, squares=squares, partner=partner
    )

    a_load = pltpu.make_async_copy(a_in, a_ref, out_sems.at[5])
    scalars = [
        pltpu.make_async_copy(seeds_in, seeds_ref, out_sems.at[6]),
        pltpu.make_async_copy(offsets_in, offsets_ref, out_sems.at[7]),
    ]
    for copy in scalars:
        copy.start()
    a_load.start()
    barrier = pltpu.get_barrier_semaphore()
    for device in peers:
        pl.semaphore_signal(barrier, inc=1, device_id=device, device_id_type=MESH)

    for copy in scalars:
        copy.wait()

    snap_ids = (
        offsets_ref[1] * (snaps * line * 2) + tm * snaps
        + lax.broadcasted_iota(jnp.int32, (1, snaps), 1)
    )
    snap_hash = scramble(snap_ids * 668265261 + seeds_ref[0])
    cell_ids = (
        offsets_ref[0] * (cells * squares) + space * cells
        + lax.broadcasted_iota(jnp.int32, (1, cells), 1)
    )
    cell_hash = scramble(cell_ids * 668265261 + seeds_ref[1])
    omega_scale = math.sqrt(3.0) / 16777216.0 / math.sqrt(cells * squares * snaps * line * 2)
    psi_scale = math.sqrt(3.0) / 16777216.0 / math.sqrt(cells * squares)

    def split_snapshots():
        a_load.wait()

        @pl.loop(0, cells // 128)
        def _(index):
            rows = pl.ds(pl.multiple_of(index * 128, 128), 128)
            a_hi[rows, :], a_lo[rows, :] = halves(a_ref[rows, :])

    half_range = half_rows // 2

    def omega(owner, turn):
        offset = turn * half_range

        @pl.loop(0, half_range // STRIP)
        def _(index):
            base = pl.multiple_of(index * STRIP, STRIP)
            ids = lax.broadcasted_iota(jnp.int32, (STRIP, snaps), 0) + (
                owner * half_rows + offset + base
            )
            strip = table_strip(snap_hash, ids, omega_scale)
            o_hi[pl.ds(base, STRIP), :], o_lo[pl.ds(base, STRIP), :] = halves(strip)

    def range_part(target, turn):
        offset = turn * half_range

        @pl.loop(0, cells // 512)
        def _(index):
            here = pl.ds(pl.multiple_of(index * 512, 512), 512)
            target[offset : offset + half_range, here] = (
                nt(o_hi[...], a_hi[here, :]) + nt(o_hi[...], a_lo[here, :])
                + nt(o_lo[...], a_hi[here, :])
            )

    def psi(lo, hi):
        @pl.loop(lo // STRIP, hi // STRIP)
        def _(index):
            base = pl.multiple_of(index * STRIP, STRIP)
            ids = lax.broadcasted_iota(jnp.int32, (STRIP, cells), 0) + base
            strip = table_strip(cell_hash, ids, psi_scale)
            p_hi[pl.ds(base, STRIP), :], p_lo[pl.ds(base, STRIP), :] = halves(strip)

    def line_copy(way, index, source):
        target = from_left if way == 0 else from_right
        return pltpu.make_async_remote_copy(
            src_ref=source, dst_ref=target.at[index], send_sem=line_sems.at[way, 0, index],
            recv_sem=line_sems.at[way, 1, index],
            device_id=right if way == 0 else left, device_id_type=MESH,
        )

    gives = []
    per_turn = CHUNKS // 2
    for turn in range(2):
        omega(1 - core, turn)
        if turn == 0:
            split_snapshots()
        range_part(give, turn)
        if turn == 0:
            pl.semaphore_wait(barrier, len(peers))
        rows = pl.ds(turn * half_range, half_range)
        copy = pltpu.make_async_remote_copy(
            src_ref=give.at[rows], dst_ref=got.at[rows], send_sem=give_sems.at[0, turn],
            recv_sem=give_sems.at[1, turn], device_id=partner, device_id_type=MESH,
        )
        copy.start()
        gives.append(copy)
        omega(core, turn)
        range_part(own_range, turn)
        copy.wait_recv()
        for index in range(turn * per_turn, (turn + 1) * per_turn):
            rows = pl.ds(index * chunk, chunk)
            yc[index] = own_range[rows, :] + got[rows, :]

            @pl.when(z == 0)
            def _():
                line_copy(0, index, yc.at[index]).start()

            @pl.when(z == line - 1)
            def _():
                line_copy(1, index, yc.at[index]).start()

    def line_step(step):
        index = step - 1 - LAG * (z - 1)

        @pl.when((z > 0) & (index >= 0) & (index < CHUNKS))
        def _():
            line_copy(0, index, yc.at[index]).wait_recv()
            from_left[index] = from_left[index] + yc[index]

            @pl.when(z < line - 1)
            def _():
                line_copy(0, index, from_left.at[index]).start()

        other = step - 1 - LAG * (line - 2 - z)

        @pl.when((z < line - 1) & (other >= 0) & (other < CHUNKS))
        def _():
            line_copy(1, other, yc.at[other]).wait_recv()

            @pl.when(z > 0)
            def _():
                to_left[other] = from_right[other] + yc[other]
                line_copy(1, other, to_left.at[other]).start()

        done = step - 1 - LAG * (line - 2)
        if 0 <= done < CHUNKS:
            rows = pl.ds(pl.multiple_of(core * half_rows + done * chunk, 8), chunk)

            @pl.when(z == 0)
            def _():
                yt[rows, :] = yc[done] + from_right[done]

            @pl.when(z == line - 1)
            def _():
                yt[rows, :] = from_left[done]

            @pl.when((z > 0) & (z < line - 1))
            def _():
                yt[rows, :] = from_left[done] + from_right[done]

    def line_drain():
        @pl.when(z < line - 1)
        def _():
            for index in range(CHUNKS):
                line_copy(0, index, yc.at[index]).wait_send()

        @pl.when(z > 0)
        def _():
            for index in range(CHUNKS):
                line_copy(1, index, yc.at[index]).wait_send()

    def corange(index):
        size = CORANGE // groups
        for start in range(index * size, (index + 1) * size, 256):
            here = pl.ds(start, 256)
            part = (
                nn(p_hi[here, :], a_hi[...]) + nn(p_hi[here, :], a_lo[...])
                + nn(p_lo[here, :], a_hi[...])
            )
            w_hi[here, :], w_lo[here, :] = halves(part)

    y_pass, shared = [], []

    def couple(group):
        first = group * group_rows
        copy = core_copy(place, yt, core * half_rows + first, group_rows, ycore_sems.at[group])
        copy.start()
        y_pass.append(copy)
        rows = pl.ds(pl.multiple_of(core * half_rows + first, 8), group_rows)
        high, low = halves(yt[rows, :])
        both = jnp.concatenate([high, low], axis=0)
        for tile in range(CORANGE // 256):
            here = pl.ds(tile * 256, 256)
            most = nt(both, p_hi[here, :])
            m_block[group, :, here] = (
                most[:group_rows] + most[group_rows:] + nt(high, p_lo[here, :])
            )
        total = Shared(
            place, m_block.at[group], m_slots.at[group], mt, first, m_sems.at[group],
            mcore_sems.at[group],
        )
        total.scatter()
        shared.append(total)

    steps = list(range(1, CHUNKS + 1 + LAG * (line - 2)))
    strips = CORANGE // 8
    for turn in range(8):
        psi(turn * strips, (turn + 1) * strips)
        if turn >= 1:
            line_step(steps.pop(0))
    tasks = []
    for group in range(groups):
        last = (group + 1) * per_group + LAG * (line - 2)
        while steps and steps[0] <= last:
            line_step(steps.pop(0))
            if tasks and group:
                tasks.pop(0)()
        couple(group)
        if group >= 1:
            tasks.append(shared[group - 1].reduce)
        tasks.append(functools.partial(corange, group))
        if group >= 2:
            tasks.append(shared[group - 2].collect)
    for group in range(groups):
        rows = (1 - core) * half_rows + group * group_rows
        core_copy(place, yt, rows, group_rows, ycore_sems.at[group]).wait_recv()
    g_rows = g_slots.shape[1]

    def g_part(index):
        return pl.ds(pl.multiple_of(core * half_rows + index * g_rows, 8), g_rows)

    g_own = g_part(z)
    g_slots[space] = nt(yt[g_own, :], yt[...], PRECISE)

    def g_square(hop, slot):
        return pltpu.make_async_remote_copy(
            src_ref=g_slots.at[slot], dst_ref=g_slots.at[slot], send_sem=g_sems.at[0, hop - 1],
            recv_sem=g_sems.at[1, hop - 1], device_id=(lax.rem(space + hop, squares), tm),
            device_id_type=MESH,
        )

    def g_line(hop, rows):
        return pltpu.make_async_remote_copy(
            src_ref=gt.at[rows], dst_ref=gt.at[rows], send_sem=gz_sems.at[0, hop - 1],
            recv_sem=gz_sems.at[1, hop - 1],
            device_id=(space, lax.rem(z + hop, line) * 2 + core), device_id_type=MESH,
        )

    g_sent = [g_square(hop, space) for hop in range(1, squares)]
    for copy in g_sent:
        copy.start()
    while tasks:
        tasks.pop(0)()
    shared[groups - 1].reduce()
    for hop in range(1, squares):
        g_square(hop, lax.rem(space + squares - hop, squares)).wait_recv()
    total = g_slots[0]
    for index in range(1, squares):
        total = total + g_slots[index]
    gt[g_own, :] = total
    for hop in range(1, line):
        copy = g_line(hop, g_own)
        copy.start()
        g_sent.append(copy)

    @pl.loop(0, cells // 128)
    def _(index):
        here = pl.ds(pl.multiple_of(index * 128, 128), 128)
        y_hi[here, :], y_lo[here, :] = halves(jnp.transpose(yt[:, here]))

    stores = [
        pltpu.make_async_copy(y_hi, yh_out, out_sems.at[0]),
        pltpu.make_async_copy(y_lo, yl_out, out_sems.at[1]),
    ]
    for copy in stores:
        copy.start()
    if groups > 1:
        shared[groups - 2].collect()
    shared[groups - 1].collect()
    for total in shared:
        total.complete()
    for lo in range(0, RANGE, 256):
        normal[lo : lo + 256, lo:] = nt(mt[lo : lo + 256, :], mt[lo:, :], PRECISE)
    def right_side(lo):
        here = pl.ds(lo, 256)
        m_hi, m_lo = halves(mt[here, :])
        rhs[here, :] = nn(m_hi, w_hi[...]) + nn(m_hi, w_lo[...]) + nn(m_lo, w_hi[...])

    for lo in range(0, RANGE, 256):
        right_side(lo)
    r_shared = Shared(place, rhs, rhs_slots, rhs_sum, 0, r_sems, None)
    r_shared.scatter()
    for hop in range(1, line):
        g_line(hop, g_part(lax.rem(z + line - hop, line))).wait_recv()
    copy = core_copy(place, gt, core * half_rows, half_rows, gcore_sems)
    copy.start()
    g_sent.append(copy)
    core_copy(place, gt, (1 - core) * half_rows, half_rows, gcore_sems).wait_recv()
    for copy in g_sent:
        copy.wait_send()

    tiles = [gt[:TILE, :TILE], normal[:TILE, :TILE]]
    for base in range(0, RANGE, TILE):
        tiles = factor_tile(base, tiles, gt, normal, inverse, factor)
        if base == TILE:
            r_shared.reduce()
    stores.append(pltpu.make_async_copy(factor, factor_out, out_sems.at[2]))
    stores[-1].start()
    r_shared.collect()
    for base in range(0, RANGE, TILE):
        here, end = slice(base, base + TILE), base + TILE
        solved = dot(inverse[here, :end], rhs_sum[:end, :])
        part = gram_dot(inverse[here, :end], solved)
        if base:
            weights[:base, :] += part[:base]
        weights[here, :] = part[base:]
    wt_hi[...], wt_lo[...] = halves(weights[...])
    for source, target, sem in ((wt_hi, wh_out, 3), (wt_lo, wl_out, 4)):
        stores.append(pltpu.make_async_copy(source, target, out_sems.at[sem]))
        stores[-1].start()

    for copy in gives + y_pass:
        copy.wait_send()
    for total in shared + [r_shared]:
        total.drain()
    line_drain()
    for copy in stores:
        copy.wait()


def sketch(snapshots, test_seeds, block_offsets):
    cells, snaps = snapshots.shape
    squares = lax.axis_size("space")
    line = lax.axis_size("tm") // 2
    half_rows = RANGE // 2
    chunk = half_rows // CHUNKS
    group_rows = max(half_rows // 4, 8 * squares)
    groups = half_rows // group_rows
    f32, bf16 = jnp.float32, jnp.bfloat16
    dma = pltpu.SemaphoreType.DMA
    scratch = [
        pltpu.SMEM((2,), jnp.int32), pltpu.SMEM((2,), jnp.int32),
        pltpu.VMEM((cells, snaps), f32),
        pltpu.VMEM((cells, snaps), bf16), pltpu.VMEM((cells, snaps), bf16),
        pltpu.VMEM((half_rows // 2, snaps), bf16), pltpu.VMEM((half_rows // 2, snaps), bf16),
        pltpu.VMEM((CORANGE, cells), bf16), pltpu.VMEM((CORANGE, cells), bf16),
        pltpu.VMEM((half_rows, cells), f32), pltpu.VMEM((half_rows, cells), f32),
        pltpu.VMEM((half_rows, cells), f32),
        pltpu.VMEM((CHUNKS, chunk, cells), f32), pltpu.VMEM((CHUNKS, chunk, cells), f32),
        pltpu.VMEM((CHUNKS, chunk, cells), f32), pltpu.VMEM((CHUNKS, chunk, cells), f32),
        pltpu.VMEM((RANGE, cells), f32), pltpu.VMEM((RANGE, CORANGE), f32),
        pltpu.VMEM((RANGE, RANGE), f32),
        pltpu.VMEM((groups, group_rows, CORANGE), f32),
        pltpu.VMEM((groups, squares - 1, group_rows // squares, CORANGE), f32),
        pltpu.VMEM((squares, half_rows // line, RANGE), f32),
        pltpu.VMEM((CORANGE, snaps), bf16), pltpu.VMEM((CORANGE, snaps), bf16),
        pltpu.VMEM((RANGE, RANGE), f32), pltpu.VMEM((RANGE, snaps), f32),
        pltpu.VMEM((squares - 1, RANGE // squares, snaps), f32), pltpu.VMEM((RANGE, snaps), f32),
        pltpu.VMEM((RANGE, RANGE), f32), pltpu.VMEM((RANGE, RANGE), f32),
        pltpu.VMEM((RANGE, snaps), f32),
        pltpu.VMEM((cells, RANGE), bf16), pltpu.VMEM((cells, RANGE), bf16),
        pltpu.VMEM((RANGE, snaps), bf16), pltpu.VMEM((RANGE, snaps), bf16),
        dma((2, 2)), dma((2, 2, CHUNKS)), dma((groups, 2)),
        dma((groups, 2, 2, squares - 1)), dma((groups, 2)),
        dma((2, squares - 1)), dma((2, line - 1)), dma((2,)), dma((2, 2, squares - 1)), dma((8,)),
    ]
    flops = 2 * 3 * cells * snaps * (RANGE + CORANGE) + 2 * 9 * RANGE * RANGE * CORANGE
    return pl.pallas_call(
        functools.partial(sketch_kernel, squares, line),
        out_shape=(
            jax.ShapeDtypeStruct((cells, RANGE), bf16),
            jax.ShapeDtypeStruct((cells, RANGE), bf16),
            jax.ShapeDtypeStruct((RANGE, RANGE), f32),
            jax.ShapeDtypeStruct((RANGE, snaps), bf16),
            jax.ShapeDtypeStruct((RANGE, snaps), bf16),
        ),
        in_specs=[
            pl.BlockSpec(memory_space=pl.ANY), pl.BlockSpec(memory_space=pl.ANY),
            pl.BlockSpec(memory_space=pl.ANY),
        ],
        out_specs=(pl.BlockSpec(memory_space=pl.ANY),) * 5,
        scratch_shapes=scratch,
        compiler_params=pltpu.CompilerParams(
            collective_id=0, has_side_effects=True, vmem_limit_bytes=40 * 1024 * 1024
        ),
        cost_estimate=pl.CostEstimate(
            flops=flops, bytes_accessed=8 * cells * snaps, transcendentals=0
        ),
        name="sketch",
    )(test_seeds, block_offsets, snapshots)


def residual_kernel(a_ref, yh_ref, yl_ref, wh_ref, wl_ref, factor_in, out_ref, factor_out):
    out_ref[...] = a_ref[...] - (
        nn(yh_ref[...], wh_ref[...]) + nn(yh_ref[...], wl_ref[...])
        + nn(yl_ref[...], wh_ref[...])
    )
    factor_out[...] = factor_in[...]


def subtract(snapshots, y_hi, y_lo, w_hi, w_lo, factor):
    cells, snaps = snapshots.shape
    tiles = 4

    def split(array):
        return pl.BlockSpec((array.shape[0] // tiles, array.shape[1]), lambda i: (i, 0))

    def whole(array):
        return pl.BlockSpec(array.shape, lambda i: (0, 0))

    return pl.pallas_call(
        residual_kernel,
        grid=(tiles,),
        out_shape=(
            jax.ShapeDtypeStruct((cells, snaps), jnp.float32),
            jax.ShapeDtypeStruct(factor.shape, jnp.float32),
        ),
        in_specs=[
            split(snapshots), split(y_hi), split(y_lo), whole(w_hi), whole(w_lo), split(factor)
        ],
        out_specs=(split(snapshots), split(factor)),
        compiler_params=pltpu.CompilerParams(vmem_limit_bytes=16 * 1024 * 1024),
        cost_estimate=pl.CostEstimate(
            flops=6 * cells * snaps * RANGE, bytes_accessed=16 * cells * snaps,
            transcendentals=0,
        ),
        name="subtract",
    )(snapshots, y_hi, y_lo, w_hi, w_lo, factor)


def local(snapshots, test_seeds, block_offsets):
    y_hi, y_lo, factor, w_hi, w_lo = sketch(snapshots, test_seeds, block_offsets)
    return subtract(snapshots, y_hi, y_lo, w_hi, w_lo, factor)


def solution(mesh):
    return jax.shard_map(
        local,
        mesh=mesh,
        in_specs=(P("space", "tm"), P(), P()),
        out_specs=(P("space", "tm"), P()),
        check_vma=False,
    )
```
